256 devices in a mesh: dp: 8 (over y, core), expert: 32 (over x, z).
Axes of the slice: x: 4, y: 4, z: 8, core: 2. Of those that a mesh axis runs over, the one named last changes fastest.
Arguments:
- tokens: bfloat16 [32768, 3072], P(('dp', 'expert')), may hold values from -6 to 6
- cotangent: bfloat16 [32768, 3072], P(('dp', 'expert')), may hold values from -0.3125 to 0.3125
- route_ids: int32 [32768, 2], P(('dp', 'expert')), may hold values from 0 to 7, all different within a row; in each aligned block of 128 rows (0 to 127, 128 to 255, ...) at most 36 rows name the same one
- route_probs: float32 [32768, 2], P(('dp', 'expert')), may hold values from 0.2 to 1
- gate_weight: bfloat16 [3072, 8192], P(None, 'expert'), may hold values from -0.109375 to 0.109375
- up_weight: bfloat16 [3072, 8192], P(None, 'expert'), may hold values from -0.109375 to 0.109375
- down_weight: bfloat16 [8192, 3072], P('expert'), may hold values from -0.0625 to 0.0625
Outputs:
- token_grad: bfloat16 [32768, 3072], P(('dp', 'expert'))
- gate_grad: bfloat16 [3072, 8192], P('dp', 'expert')
- up_grad: bfloat16 [3072, 8192], P('dp', 'expert')
- down_grad: bfloat16 [8192, 3072], P('expert', 'dp')
The draws below stay inside these ranges and needn't reach their ends.
Inputs may be any that keep to these rules, and one draw needn't show every extreme that they name: `route_ids`: in every block of 128 consecutive tokens (the tokens of one device) at most 36 tokens name any one expert, a bound that some block reaches; a token's 2 ids differ.
All inputs are finite; a program needn't handle non-finite values.
Results may differ from the reference program's by a relative error of at most 0.023.
Values may be sent and summed in bfloat16 or wider, within the bound.
A program may use at most 128 MiB of HBM per device.

```python
import math
import jax
import jax.numpy as jnp
import numpy as np
from jax import lax

D = 3072
HID = 8192
EXPERTS = 8
TOP = 2
TOK_DEV = 128
CAP = 36
HID_DEV = 256
TOKENS = 32768
N_DP = 8
N_EXPERT = 32


def shard_levels(own_key, extent, split, low, top_value):
    def one(dim, blocks):
        heights = jax.random.uniform(jax.random.fold_in(jax.random.fold_in(own_key, 6), dim), (blocks,), jnp.float32, low / len(split), top_value / len(split))
        return jnp.repeat(jnp.exp(heights), extent[dim] // blocks).reshape((-1,) + (1,) * (len(extent) - dim - 1))

    loudness = one(*split[0])
    for cut in split[1:]:
        loudness = loudness * one(*cut)
    return loudness


def assign_block(stream_key, own, number, rows, count, top, most, skew):
    order = jax.random.permutation(stream_key, count)
    heavy_load, ordinary = load_shares(count, rows * top, most, skew, True), load_shares(count, rows * top, most, skew, False)
    places = jnp.arange(count)

    def named(tallies, offset_by):
        used = int((tallies > 0).sum())
        fixed = max(1, used // 4)
        shifted = fixed + (places - fixed + offset_by * (used - fixed)) % max(1, count - fixed)
        return jnp.zeros((count,), jnp.int32).at[order[jnp.where(places < fixed, places, shifted)]].set(jnp.asarray(tallies, jnp.int32))

    tallies = jnp.where(number % 4 == 0, named(heavy_load, number // 4), named(ordinary, number - number // 4 - 1))
    mixed = jax.random.permutation(jax.random.fold_in(own, 3), count)
    source_of, sink = mixed[0:count // 2 * 2:2], mixed[1:count // 2 * 2:2]
    room = jnp.minimum(tallies[source_of] - 1, most - tallies[sink]) // 2
    room = jnp.where((source_of == order[0]) | (sink == order[0]) | (tallies[sink] == 0), 0, jnp.maximum(room, 0))
    shifted = jax.random.randint(jax.random.fold_in(own, 4), (count // 2,), 0, 1 << 20) % (room + 1)
    tallies = tallies.at[source_of].add(-shifted).at[sink].add(shifted)
    items = jnp.searchsorted(jnp.cumsum(tallies), jnp.arange(rows * top), side="right").astype(jnp.int32)
    listing = items.reshape(top, rows).T
    listing = listing[jax.random.permutation(jax.random.fold_in(own, 1), rows)]
    offset_by = jax.random.randint(jax.random.fold_in(own, 2), (rows, 1), 0, top)
    return jnp.take_along_axis(listing, (jnp.arange(top)[None, :] + offset_by) % top, axis=1)


def load_shares(count, total, bound, lean, full):
    loads = [(1 << 20) // math.isqrt(standing ** lean) + 1 for standing in range(1, count + 1)]
    largest = bound if full else min(bound, max(-(-total // count), total * loads[0] // sum(loads)))
    least = 1 if total - largest >= count - 1 else 0
    holding, surplus = [largest] + [least] * (count - 1), total - largest - least * (count - 1)
    while surplus > 0:
        candidates = [i for i in range(1, count) if holding[i] < largest] or [i for i in range(1, count) if holding[i] < bound]
        pool, remaining = sum([loads[i] for i in candidates]), surplus
        for i in candidates:
            more = min(bound - holding[i], max(1, remaining * loads[i] // pool), surplus)
            holding[i] = holding[i] + more
            surplus = surplus - more
    return np.array(holding)


def gaussian(key, shape, deviation, most, shards=(), held_as=jnp.bfloat16):
    entries = deviation * jax.random.normal(key, shape, jnp.float32)
    if shards:
        entries = entries * shard_levels(key, shape, shards, -0.22, 0.18)
    return jnp.clip(entries, -most, most).astype(held_as)


def setup_inputs(seed: int = 0) -> dict:
    key_of = jax.random.split(jax.random.key(seed), 8)
    tokens = gaussian(key_of[0], (TOKENS, D), 1.0, 6.0, ((0, 256),))
    cotangent = gaussian(key_of[1], (TOKENS, D), 0.05, 0.3125, ((0, 256),))
    route_ids_keys = jax.random.split(jax.random.fold_in(key_of[2], 1), TOKENS // TOK_DEV)
    route_ids_turns = jax.random.permutation(jax.random.fold_in(key_of[2], 3), TOKENS // TOK_DEV)
    route_ids = jax.vmap(lambda own, number: assign_block(jax.random.fold_in(key_of[2], 2), own, number, TOK_DEV, EXPERTS, TOP, CAP, 2))(route_ids_keys, route_ids_turns).reshape((TOKENS, TOP))
    route_probs = jnp.clip(0.2 + 0.8 * jax.random.uniform(key_of[3], (TOKENS, TOP), jnp.float32) ** shard_levels(key_of[3], (TOKENS, TOP), ((0, 256),), -0.2, 0.2), 0.2, 1.0)
    gate_weight = gaussian(key_of[4], (D, HID), D ** -0.5, 0.109375, ((1, 32),))
    up_weight = gaussian(key_of[5], (D, HID), D ** -0.5, 0.109375, ((1, 32),))
    down_weight = gaussian(key_of[6], (HID, D), HID ** -0.5, 0.0625, ((0, 32),))
    return dict(tokens=tokens, cotangent=cotangent, route_ids=route_ids, route_probs=route_probs, gate_weight=gate_weight, up_weight=up_weight, down_weight=down_weight)


def compact(block_tokens, block_cotan, block_ids, block_probs):
    hits = block_ids == 0
    chosen = jnp.any(hits, axis=1).astype(jnp.int32)
    share = jnp.sum(jnp.where(hits, block_probs, 0.0), axis=1).astype(jnp.float32)
    slots = (jnp.cumsum(chosen) - chosen).astype(jnp.int32)
    placer = ((slots[:, None] == jnp.arange(CAP, dtype=jnp.int32)[None, :]) & (chosen[:, None] == 1)).astype(jnp.float32)
    rows = jnp.dot(placer.T, block_tokens.astype(jnp.float32), precision=lax.Precision.HIGHEST).astype(jnp.bfloat16)
    cotan_rows = jnp.dot(placer.T, block_cotan.astype(jnp.float32), precision=lax.Precision.HIGHEST).astype(jnp.bfloat16)
    shares = jnp.sum(placer * share[:, None], axis=0)
    return rows, cotan_rows, shares, placer


def rounded(value):
    return lax.optimization_barrier(value.astype(jnp.bfloat16)).astype(jnp.float32)


def reference(tokens, cotangent, route_ids, route_probs, gate_weight, up_weight, down_weight):
    width = tokens.shape[1]
    grid_tokens = tokens.reshape(N_DP, N_EXPERT, TOK_DEV, width)
    grid_cotan = cotangent.reshape(N_DP, N_EXPERT, TOK_DEV, width)
    grid_ids = route_ids.reshape(N_DP, N_EXPERT, TOK_DEV, TOP)
    grid_probs = route_probs.reshape(N_DP, N_EXPERT, TOK_DEV, TOP)
    rows, cotan_rows, shares, placer = jax.vmap(jax.vmap(compact))(grid_tokens, grid_cotan, grid_ids, grid_probs)
    total_rows = N_EXPERT * CAP
    rows = rows.reshape(N_DP, total_rows, width)
    cotan_rows = cotan_rows.reshape(N_DP, total_rows, width)
    shares = shares.reshape(N_DP, total_rows)
    slice_gate = gate_weight.reshape(width, N_EXPERT, HID_DEV).transpose(1, 0, 2)
    slice_up = up_weight.reshape(width, N_EXPERT, HID_DEV).transpose(1, 0, 2)

    def row_pass(carry, inputs):
        gate_sum, up_sum, down_sum = carry
        row_block, cotan_block, share_block = inputs
        gate_pre = jnp.dot(row_block, gate_weight, preferred_element_type=jnp.float32)
        up_pre = jnp.dot(row_block, up_weight, preferred_element_type=jnp.float32)
        sigma = jax.nn.sigmoid(gate_pre)
        gate_act = gate_pre * sigma
        hidden = (gate_act * up_pre).astype(jnp.bfloat16)
        scaled = (share_block[:, None] * cotan_block.astype(jnp.float32)).astype(jnp.bfloat16)
        down_part = jnp.dot(hidden.T, scaled, preferred_element_type=jnp.float32)
        hidden_back = jnp.dot(scaled, down_weight.T, preferred_element_type=jnp.float32)
        gate_back = (hidden_back * up_pre * sigma * (1.0 + gate_pre * (1.0 - sigma))).astype(jnp.bfloat16)
        up_back = (hidden_back * gate_act).astype(jnp.bfloat16)
        gate_part = jnp.dot(row_block.T, gate_back, preferred_element_type=jnp.float32)
        up_part = jnp.dot(row_block.T, up_back, preferred_element_type=jnp.float32)
        gate_slices = gate_back.reshape(total_rows, N_EXPERT, HID_DEV).transpose(1, 0, 2)
        up_slices = up_back.reshape(total_rows, N_EXPERT, HID_DEV).transpose(1, 0, 2)

        def slice_term(total, pieces):
            gate_piece, up_piece, gate_cols, up_cols = pieces
            term = jnp.dot(gate_piece, gate_cols.T, preferred_element_type=jnp.float32)
            term = term + jnp.dot(up_piece, up_cols.T, preferred_element_type=jnp.float32)
            return total + rounded(term), None

        start = jnp.zeros((total_rows, width), jnp.float32)
        back_rows, _ = lax.scan(slice_term, start, (gate_slices, up_slices, slice_gate, slice_up))
        carry = (gate_sum + rounded(gate_part), up_sum + rounded(up_part), down_sum + rounded(down_part))
        return carry, back_rows

    empty_in = jnp.zeros((width, HID), jnp.float32)
    empty_down = jnp.zeros((HID, width), jnp.float32)
    sums, back_all = lax.scan(row_pass, (empty_in, empty_in, empty_down), (rows, cotan_rows, shares))
    back_all = back_all.reshape(N_DP, N_EXPERT, CAP, width)
    placed = jnp.einsum("abtc,abcd->abtd", placer, back_all, precision=lax.Precision.HIGHEST)
    token_grad = placed.reshape(TOKENS, width).astype(jnp.bfloat16)
    return token_grad, sums[0].astype(jnp.bfloat16), sums[1].astype(jnp.bfloat16), sums[2].astype(jnp.bfloat16)
```

```python
import functools
import heapq

import jax
import jax.numpy as jnp
from jax import lax
from jax.experimental import pallas as pl
from jax.experimental.pallas import tpu as pltpu
from jax.sharding import PartitionSpec as P

CAP = 36
ROWS = 32
PACK = 8
EXTRA = CAP - ROWS
TOK = 128
D = 3072
H = 256
CA = 1280
CB = D - CA
NX, NZ, NY = 4, 8, 4
SH = D // 8
BF = jnp.bfloat16
F32 = jnp.float32
LINK_RATE = 46e3
CORE_RATE = 250e3
LATENCY = 1.6

REACH = {
    0: {"x": (2, 1), "z": (4, 3)},
    1: {"x": (1, 2), "z": (3, 4)},
}
SIZE = {"x": NX, "z": NZ, "y": NY}
RS_COLS = {
    ("A", 0): (0, CA // 2),
    ("A", 1): (CA // 2, CA // 2),
    ("B", 0): (CA, CB // 2),
    ("B", 1): (CA + CB // 2, CB // 2),
}


class Msg:
    def __init__(self, link, size, src, dst):
        self.link, self.size, self.src, self.dst = link, size, src, dst


class Task:
    def __init__(self, name, deps, sends=(), dur=0.0, rank=0, emit=None):
        self.name, self.deps, self.sends = name, tuple(deps), list(sends)
        self.dur, self.rank, self.emit = dur, rank, emit


GROUP = NX * CAP


def row_of(dz, dx):
    return dz * GROUP + dx * ROWS


def pack_of(dz, dx):
    return (dz * NX + dx) * PACK


def plan():
    msgs, tasks = {}, []

    first_sends, hold = [], []
    by_dz = {dz: [] for dz in range(NZ)}
    for kind, f, g, cols in (("A", "x", "z", CA), ("B", "z", "x", CB)):
        for tw in (0, 1):
            def at(cf, cg):
                dx, dz = (cf, cg) if f == "x" else (cg, cf)
                return dz % NZ, dx % NX

            def send(cf, cg, axis, up):
                step = -1 if up else 1
                nf, ng = (cf + step, cg) if axis == f else (cf, cg + step)
                dst = at(nf, ng)
                link = axis + ("+" if up else "-")
                keys = []
                for what, name, size in (("G", "ag", ROWS * cols), ("E", "age", PACK * cols // 2)):
                    key = (name, kind, tw) + dst
                    msgs[key] = Msg(link, size * 2, (what, kind, tw) + at(cf, cg), (what, kind, tw) + dst)
                    keys.append(key)
                by_dz[dst[0]].extend(keys)
                return keys

            def visit(cf, cg, via, up, hops):
                out = []
                if via in (None, f):
                    for u in (True, False):
                        reach = REACH[tw][f][0 if u else 1]
                        if via is None or (u == up and hops < reach):
                            out.append((send(cf, cg, f, u), cf + (-1 if u else 1), cg, f, u, 1 if via is None else hops + 1))
                    for u in (True, False):
                        out.append((send(cf, cg, g, u), cf, cg + (-1 if u else 1), g, u, 1))
                elif hops < REACH[tw][g][0 if up else 1]:
                    out.append((send(cf, cg, g, up), cf, cg + (-1 if up else 1), g, up, hops + 1))
                if via is None:
                    first_sends.extend(k for o in out for k in o[0])
                elif out:
                    here = (kind, tw) + at(cf, cg)
                    sends = [k for o in out for k in o[0]]
                    tasks.append(Task(("fwd",) + here, [("ag",) + here, ("age",) + here], sends, 0.05, 0))
                    if any(msgs[k].link[0] == "x" for k in sends):
                        hold.append(("fwd",) + here)
                for key, a, b, v, u, h in out:
                    visit(a, b, v, u, h)

            visit(0, 0, None, None, 0)
    tasks.append(Task("pick", [], first_sends, 2.0, 0, ("pick",)))

    for dz in range(NZ):
        tasks.append(Task(("main", dz), ["pick", "weights"] + by_dz[dz], [], 3.0, 3, ("main", dz)))
    tasks.append(Task("weights", ["pick"], [], 0.1, 1, ("weights",)))
    task_of = {t.name: t for t in tasks}

    def chain(kind, tw, axis, up, fixed, at_of, blocks, ready, packed=False):
        c0, cols = RS_COLS[kind, tw]
        what, nrows = "P", ROWS * blocks
        if packed:
            what, nrows, c0, cols = "P" + kind, PACK * blocks, 0, (CA if kind == "A" else CB) // 2
        reach = REACH[tw][axis][0 if up else 1]
        sign = 1 if up else -1
        prev = None
        for k in range(reach, -1, -1):
            here = (sign * k) % SIZE[axis]
            r0 = pack_of(*at_of(here)) if packed else row_of(*at_of(here))
            name = ("rs", kind, tw, axis, up, fixed, packed, k)
            key = ("rsm", kind, tw, axis, up, fixed, packed, k - 1)
            deps = list(ready(here))
            if prev is not None:
                deps.append(prev)
            sends = []
            if k > 0:
                msgs[key] = Msg(
                    axis + ("+" if up else "-"), nrows * cols * 2, (what, r0, nrows, c0, cols), ("R", key, nrows, cols)
                )
                sends = [key]
            emit = None if prev is None else ("add", prev, what, r0, nrows, c0, cols)
            dur = 0.0 if prev is None else 0.1 + nrows * cols * 2 / 1.5e6
            tasks.append(Task(name, deps, sends, dur, 1 if k else 2, emit))
            prev = key
        return name

    ends = []
    for tw, packed in ((0, False), (1, False), (0, True), (1, True)):
        if not (packed and tw == 1):
            za = {
                p: [
                    chain("A", tw, "z", up, p, lambda h, p=p: (h, p), 2, lambda h: [("main", h)], packed)
                    for up in (True, False)
                ]
                for p in (2, 0)
            }
            ends += [
                chain("A", tw, "x", up, 0, lambda h: (0, h), 1, lambda h: za[h // 2 * 2], packed)
                for up in (True, False)
            ]
        if packed and tw == 0:
            continue
        xb = {}
        for dz in (4, 3, 5, 2, 6, 1, 7, 0):
            xb[dz] = [
                chain(
                    "B", tw, "x", up, dz, lambda h, dz=dz: (dz, h), 1, lambda h, dz=dz: [("main", dz)] + hold, packed
                )
                for up in (True, False)
            ]
        ends += [
            chain("B", tw, "z", up, 0, lambda h: (h, 0), 1, lambda h: xb[h], packed)
            for up in (True, False)
        ]
    tasks.append(Task("final", ends, [], 1.5, 5, ("final",)))

    mains = [("main", dz) for dz in range(NZ)]
    tasks.append(Task("turn", mains, [], 1.5, 4, ("turn",)))
    last = "turn"
    for i, (kind, lo, hi) in enumerate((("A", 0, 2), ("A", 2, 5), ("B", 0, 2), ("B", 2, 4), ("B", 4, 7))):
        tasks.append(Task(("grad", i), [last], [], 0.9 * (hi - lo), 4, ("grad", kind, lo, hi)))
        last = ("grad", i)
    for dy in (2, 3, 1, 0):
        key = ("cx", dy)
        msgs[key] = Msg("core", 3 * H * SH * 2, ("W", dy, True, 0, 3 * H), ("CX", dy))
        task_of_last = tasks[-1]
    grad_end = tasks[-1]
    grad_end.sends = [("cx", dy) for dy in (2, 3, 1, 0)]
    for dy in range(NY):
        tasks.append(Task(("cadd", dy), [last, ("cx", dy)], [], 0.6, 2, ("cadd", dy)))
    dp_ends = []
    half = 3 * H // 2
    for tw in (0, 1):
        for up in (True, False):
            reach = REACH[tw]["x"][0 if up else 1]
            prev = None
            for k in range(reach, -1, -1):
                dy = (k if up else -k) % NY
                name = ("y", tw, up, k)
                key = ("ym", tw, up, k - 1)
                deps = [("cadd", dy)] + ([prev] if prev else [])
                sends = []
                if k > 0:
                    msgs[key] = Msg(
                        "y" + ("+" if up else "-"), half * SH * 2, ("W", dy, False, tw * half, half), ("Y", key)
                    )
                    sends = [key]
                emit = None if prev is None else ("yadd", prev, dy, tw * half, half)
                tasks.append(Task(name, deps, sends, 0.0 if prev is None else 0.4, 2, emit))
                prev = key
            dp_ends.append(name)
    tasks.append(Task("wout", dp_ends, [], 1.0, 5, ("wout",)))
    return msgs, schedule(msgs, tasks)


def schedule(msgs, tasks):
    waiting = {i: set(t.deps) for i, t in enumerate(tasks)}
    users = {}
    for i, t in enumerate(tasks):
        for d in t.deps:
            users.setdefault(d, []).append(i)
    ready, arrivals, free, now, order = [], [], {}, 0.0, []
    times = {}

    def satisfy(key):
        for i in users.get(key, ()):
            waiting[i].discard(key)
            if not waiting[i]:
                heapq.heappush(ready, (tasks[i].rank, i))

    for i in range(len(tasks)):
        if not waiting[i]:
            heapq.heappush(ready, (tasks[i].rank, i))
    seq = 0
    while ready or arrivals:
        while arrivals and arrivals[0][0] <= now:
            satisfy(heapq.heappop(arrivals)[2])
        if not ready:
            now = arrivals[0][0]
            continue
        _, i = heapq.heappop(ready)
        t = tasks[i]
        now += t.dur
        order.append(t)
        times[t.name] = now
        for key in t.sends:
            m = msgs[key]
            start = max(now, free.get(m.link, 0.0))
            rate = CORE_RATE if m.link == "core" else LINK_RATE
            free[m.link] = start + m.size / rate
            seq += 1
            heapq.heappush(arrivals, (free[m.link] + LATENCY, seq, key))
        satisfy(t.name)
    if len(order) != len(tasks):
        raise ValueError("stuck")
    plan.times, plan.end = times, now
    return order


MSGS, ORDER = plan()
KEYS = sorted(MSGS, key=repr)
INDEX = {k: i for i, k in enumerate(KEYS)}
R_SLOT, R_COUNT = {}, {}
for _k in KEYS:
    if _k[0] == "rsm":
        _, _, _nr, _nc = MSGS[_k].dst
        R_SLOT[_k] = R_COUNT.get((_nr, _nc), 0)
        R_COUNT[_nr, _nc] = R_SLOT[_k] + 1
R_SHAPES = sorted(R_COUNT)
Y_KEYS = [k for k in KEYS if k[0] == "ym"]


def kernel(ids, probs, tokens, cot, wg_hbm, wu_hbm, wd_hbm, ret_out, across_out, w_out,
           ga0, ga1, gb0, gb1, ea0, ea1, eb0, eb1, part, pa, pb, wg, wu, wd, gback, uback, hid, turned, w3, cx, yr, *rest):
    landing = dict(zip(R_SHAPES, rest[: len(R_SHAPES)]))
    wsem, send_sem, recv_sem = rest[len(R_SHAPES):]
    gathered = {("A", 0): ga0, ("A", 1): ga1, ("B", 0): gb0, ("B", 1): gb1}
    extras = {("A", 0): ea0, ("A", 1): ea1, ("B", 0): eb0, ("B", 1): eb1}
    sums = {"P": part, "PA": pa, "PB": pb}

    e = lax.axis_index("expert")
    d = lax.axis_index("dp")
    x, z, y, c = e // NZ, e % NZ, d // 2, d % 2
    peer = {
        "z+": {"expert": x * NZ + (z + 1) % NZ},
        "z-": {"expert": x * NZ + (z + NZ - 1) % NZ},
        "x+": {"expert": ((x + 1) % NX) * NZ + z},
        "x-": {"expert": ((x + NX - 1) % NX) * NZ + z},
        "y+": {"dp": ((y + 1) % NY) * 2 + c},
        "y-": {"dp": ((y + NY - 1) % NY) * 2 + c},
        "core": {"dp": y * 2 + 1 - c},
    }
    loads = [
        pltpu.make_async_copy(src, dst, wsem.at[i])
        for i, (src, dst) in enumerate(((wg_hbm, wg), (wu_hbm, wu), (wd_hbm, wd)))
    ]
    for load in loads:
        load.start()
    barrier = pltpu.get_barrier_semaphore()
    for target in peer.values():
        pl.semaphore_signal(barrier, inc=1, device_id=target, device_id_type=pl.DeviceIdType.MESH)

    def shard(dy, other):
        owner = ((y + dy) % NY) * 2 + (1 - c if other else c)
        return pl.ds(pl.multiple_of(owner * SH, 128), SH)

    def ref_of(place):
        what = place[0]
        if what == "G":
            _, kind, tw, dz, dx = place
            return gathered[kind, tw].at[pl.ds(row_of(dz, dx), ROWS), :]
        if what == "E":
            _, kind, tw, dz, dx = place
            return extras[kind, tw].at[pl.ds(pack_of(dz, dx), PACK), :]
        if what in sums:
            _, r0, nr, c0, nc = place
            return sums[what].at[pl.ds(r0, nr), pl.ds(c0, nc)]
        if what == "R":
            _, key, nr, nc = place
            return landing[nr, nc].at[R_SLOT[key]]
        if what == "W":
            _, dy, other, r0, nr = place
            return w3.at[pl.ds(r0, nr), shard(dy, other)]
        if what == "CX":
            return cx.at[place[1]]
        return yr.at[Y_KEYS.index(place[1])]

    copies = {}

    def copy_of(key):
        if key not in copies:
            m = MSGS[key]
            copies[key] = pltpu.make_async_remote_copy(
                src_ref=ref_of(m.src),
                dst_ref=ref_of(m.dst),
                send_sem=send_sem.at[INDEX[key]],
                recv_sem=recv_sem.at[INDEX[key]],
                device_id=peer[m.link],
                device_id_type=pl.DeviceIdType.MESH,
            )
        return copies[key]

    def pick():
        hits = ids[...] == 0
        chosen = jnp.sum(jnp.where(hits, 1.0, 0.0), axis=0, keepdims=True)
        share = jnp.sum(jnp.where(hits, probs[...], 0.0), axis=0, keepdims=True)
        above = lax.broadcasted_iota(jnp.int32, (TOK, TOK), 0) < lax.broadcasted_iota(jnp.int32, (TOK, TOK), 1)
        wide = jnp.broadcast_to(chosen, (TOK, TOK))
        slot = jnp.dot(
            wide.astype(BF), jnp.where(above, 1.0, 0.0).astype(BF), preferred_element_type=F32
        )
        row = lax.broadcasted_iota(jnp.int32, (TOK, TOK), 0).astype(F32)
        whole = jnp.where((slot == row) & (wide > 0.5), 1.0, 0.0)
        across_out[...] = whole[: ROWS + PACK].astype(BF)
        low = whole[ROWS : ROWS + PACK]
        r8 = lax.broadcasted_iota(jnp.int32, (PACK, TOK), 0)
        wanted = (r8 + (ROWS - EXTRA)).astype(F32)
        high = jnp.where((slot[:PACK] == wanted) & (wide[:PACK] > 0.5) & (r8 >= EXTRA), 1.0, 0.0)
        maps = [whole[:ROWS], low, high]
        shares = [jnp.sum(m * share, axis=1, keepdims=True) for m in maps]
        maps = [m.astype(BF) for m in maps]

        def take(k, source, c0, cols, scale):
            got = jnp.dot(maps[k], source[:, pl.ds(c0, cols)], preferred_element_type=F32)
            return got * shares[k] if scale else got

        for c0, cols, kind in ((0, CA, "A"), (CA, CB, "B")):
            for tw, source in ((0, tokens), (1, cot)):
                gathered[kind, tw][pl.ds(0, ROWS), :] = take(0, source, c0, cols, tw == 1).astype(BF)
                extras[kind, tw][pl.ds(0, PACK), :] = (
                    take(1, source, c0, cols // 2, tw == 1) + take(2, source, c0 + cols // 2, cols // 2, tw == 1)
                ).astype(BF)
        pl.semaphore_wait(barrier, len(peer))

    def spread(high, shape, axis):
        i = lax.broadcasted_iota(jnp.int32, shape, axis)
        j = lax.broadcasted_iota(jnp.int32, shape, 1 - axis)
        return jnp.where((i >> 2) * PACK + (i & 3) + (EXTRA if high else 0) == j, 1.0, 0.0).astype(BF)

    def weights():
        for load in loads:
            load.wait()

    nt = (((1,), (1,)), ((), ()))

    def main(dz):
        rows = pl.ds(row_of(dz, 0), GROUP)
        tail = pl.ds(row_of(dz, 0) + NX * ROWS, NX * EXTRA)
        packed = pl.ds(pack_of(dz, 0), NX * PACK)
        for kind, cols in (("A", CA // 2), ("B", CB // 2)):
            for tw in (0, 1):
                for high in (0, 1):
                    gathered[kind, tw][tail, pl.ds(high * cols, cols)] = jnp.dot(
                        spread(high, (NX * EXTRA, NX * PACK), 0), extras[kind, tw][packed, :],
                        preferred_element_type=F32,
                    ).astype(BF)
        ra, rb, sa, sb = ga0[rows, :], gb0[rows, :], ga1[rows, :], gb1[rows, :]
        gate = jnp.dot(ra, wg[pl.ds(0, CA), :], preferred_element_type=F32) + jnp.dot(
            rb, wg[pl.ds(CA, CB), :], preferred_element_type=F32
        )
        up = jnp.dot(ra, wu[pl.ds(0, CA), :], preferred_element_type=F32) + jnp.dot(
            rb, wu[pl.ds(CA, CB), :], preferred_element_type=F32
        )
        back = lax.dot_general(sa, wd[:, pl.ds(0, CA)], nt, preferred_element_type=F32) + lax.dot_general(
            sb, wd[:, pl.ds(CA, CB)], nt, preferred_element_type=F32
        )
        sigma = jax.nn.sigmoid(gate)
        act = gate * sigma
        hid[rows, :] = (act * up).astype(BF)
        gb = (back * up * sigma * (1.0 + gate * (1.0 - sigma))).astype(BF)
        ub = (back * act).astype(BF)
        gback[rows, :] = gb
        uback[rows, :] = ub
        for c0 in range(0, D, 256):
            cols = pl.ds(c0, 256)
            part[rows, cols] = (
                lax.dot_general(gb, wg[cols, :], nt, preferred_element_type=F32)
                + lax.dot_general(ub, wu[cols, :], nt, preferred_element_type=F32)
            ).astype(BF)

        for out, c0, cols in ((pa, 0, CA // 2), (pb, CA, CB // 2)):
            out[packed, :] = sum(
                jnp.dot(
                    spread(high, (NX * PACK, NX * EXTRA), 1), part[tail, pl.ds(c0 + high * cols, cols)],
                    preferred_element_type=F32,
                )
                for high in (0, 1)
            ).astype(BF)

    def add(key, what, r0, nr, c0, nc):
        got = landing[nr, nc].at[R_SLOT[key]]
        here = (pl.ds(r0, nr), pl.ds(c0, nc))
        sums[what][here] = sums[what][here] + got[...]

    def turn():
        turned[pl.ds(0, H), :] = jnp.transpose(gback[...])
        turned[pl.ds(H, H), :] = jnp.transpose(uback[...])
        turned[pl.ds(2 * H, H), :] = jnp.transpose(hid[...])

    def grad(kind, lo, hi):
        base = 0 if kind == "A" else CA
        first, second = gathered[kind, 0], gathered[kind, 1]

        @pl.loop(lo, hi)
        def _(i):
            cols = pl.ds(pl.multiple_of(i * 256, 256), 256)
            out = pl.ds(pl.multiple_of(base + i * 256, 256), 256)
            w3[pl.ds(0, 2 * H), out] = jnp.dot(
                turned[pl.ds(0, 2 * H), :], first[:, cols], preferred_element_type=F32
            ).astype(BF)
            w3[pl.ds(2 * H, H), out] = jnp.dot(
                turned[pl.ds(2 * H, H), :], second[:, cols], preferred_element_type=F32
            ).astype(BF)

    def cadd(dy):
        here = shard(dy, False)
        w3[:, here] = w3[:, here] + cx[dy]

    def yadd(key, dy, r0, nr):
        here = (pl.ds(r0, nr), shard(dy, False))
        w3[here] = w3[here] + yr[Y_KEYS.index(key)]

    def final():
        ret_out[pl.ds(0, ROWS), :] = part[pl.ds(0, ROWS), :]
        for packed, c0, cols in ((pa, 0, CA // 2), (pb, CA, CB // 2)):
            for high in (0, 1):
                ret_out[pl.ds(ROWS, PACK), pl.ds(c0 + high * cols, cols)] = jnp.dot(
                    spread(high, (PACK, NX * PACK), 0), packed[pl.ds(0, NX * PACK), :],
                    preferred_element_type=F32,
                ).astype(BF)

    def wout():
        w_out[...] = w3[:, shard(0, False)]

    run = dict(pick=pick, weights=weights, main=main, add=add, turn=turn, grad=grad,
               cadd=cadd, yadd=yadd, final=final, wout=wout)
    arrived = set()
    for task in ORDER:
        for dep in task.deps:
            if dep in MSGS and dep not in arrived:
                copy_of(dep).wait_recv()
                arrived.add(dep)
        if task.emit is not None:
            run[task.emit[0]](*task.emit[1:])
        for key in task.sends:
            copy_of(key).start()
    for key in KEYS:
        copy_of(key).wait_send()


def per_device(tokens, cotangent, route_ids, route_probs, gate_weight, up_weight, down_weight):
    vmem = pl.BlockSpec(memory_space=pltpu.VMEM)
    anywhere = pl.BlockSpec(memory_space=pl.ANY)
    rows, packs = NZ * GROUP, NZ * NX * PACK
    scratch = [
        pltpu.VMEM((rows, CA), BF), pltpu.VMEM((rows, CA), BF),
        pltpu.VMEM((rows, CB), BF), pltpu.VMEM((rows, CB), BF),
        pltpu.VMEM((packs, CA // 2), BF), pltpu.VMEM((packs, CA // 2), BF),
        pltpu.VMEM((packs, CB // 2), BF), pltpu.VMEM((packs, CB // 2), BF),
        pltpu.VMEM((rows, D), BF),
        pltpu.VMEM((packs, CA // 2), BF), pltpu.VMEM((packs, CB // 2), BF),
        pltpu.VMEM((D, H), BF), pltpu.VMEM((D, H), BF), pltpu.VMEM((H, D), BF),
        pltpu.VMEM((rows, H), BF), pltpu.VMEM((rows, H), BF), pltpu.VMEM((rows, H), BF),
        pltpu.VMEM((3 * H, rows), BF),
        pltpu.VMEM((3 * H, D), BF),
        pltpu.VMEM((NY, 3 * H, SH), BF),
        pltpu.VMEM((len(Y_KEYS), 3 * H // 2, SH), BF),
    ]
    scratch += [pltpu.VMEM((R_COUNT[s],) + s, BF) for s in R_SHAPES]
    scratch += [
        pltpu.SemaphoreType.DMA((3,)),
        pltpu.SemaphoreType.DMA((len(KEYS),)),
        pltpu.SemaphoreType.DMA((len(KEYS),)),
    ]
    returned, across, grads = pl.pallas_call(
        kernel,
        out_shape=(
            jax.ShapeDtypeStruct((ROWS + PACK, D), BF),
            jax.ShapeDtypeStruct((ROWS + PACK, TOK), BF),
            jax.ShapeDtypeStruct((3 * H, SH), BF),
        ),
        in_specs=[vmem, vmem, vmem, vmem, anywhere, anywhere, anywhere],
        out_specs=(vmem, vmem, vmem),
        scratch_shapes=scratch,
        compiler_params=pltpu.CompilerParams(
            collective_id=0, has_side_effects=True, vmem_limit_bytes=67043328
        ),
    )(route_ids.T, route_probs.T, tokens, cotangent, gate_weight, up_weight, down_weight)
    token_grad = lax.dot_general(
        across, returned, (((0,), (0,)), ((), ())), preferred_element_type=F32
    ).astype(BF)
    return token_grad, grads[:H].T, grads[H : 2 * H].T, grads[2 * H :]


def solution(mesh):
    in_specs = (
        P(("dp", "expert"), None),
        P(("dp", "expert"), None),
        P(("dp", "expert"), None),
        P(("dp", "expert"), None),
        P(None, "expert"),
        P(None, "expert"),
        P("expert", None),
    )
    out_specs = (P(("dp", "expert"), None), P("dp", "expert"), P("dp", "expert"), P("expert", "dp"))
    return jax.shard_map(
        per_device, mesh=mesh, in_specs=in_specs, out_specs=out_specs, check_vma=False
    )
```

```python
import functools
import heapq

import jax
import jax.numpy as jnp
from jax import lax
from jax.experimental import pallas as pl
from jax.experimental.pallas import tpu as pltpu
from jax.sharding import PartitionSpec as P

CAP = 36
ROWS = 32
PACK = 8
EXTRA = CAP - ROWS
TOK = 128
D = 3072
H = 256
CA = 1280
CB = D - CA
NX, NZ, NY = 4, 8, 4
SH = D // 8
UNITS = ((0, 2 * H), (2 * H, H))
BF = jnp.bfloat16
F32 = jnp.float32
LINK_RATE = 46e3
CORE_RATE = 250e3
LATENCY = 1.6

REACH = {
    0: {"x": (2, 1), "z": (4, 3)},
    1: {"x": (1, 2), "z": (3, 4)},
}
SIZE = {"x": NX, "z": NZ, "y": NY}
RS_COLS = {
    ("A", 0): (0, CA // 2),
    ("A", 1): (CA // 2, CA // 2),
    ("B", 0): (CA, CB // 2),
    ("B", 1): (CA + CB // 2, CB // 2),
}


class Msg:
    def __init__(self, link, size, src, dst):
        self.link, self.size, self.src, self.dst = link, size, src, dst


class Task:
    def __init__(self, name, deps, sends=(), dur=0.0, rank=0, emit=None):
        self.name, self.deps, self.sends = name, tuple(deps), list(sends)
        self.dur, self.rank, self.emit = dur, rank, emit


GROUP = NX * CAP


PLACE = {dz: i for i, dz in enumerate((0, 1, 7, 2, 6, 3, 5, 4))}
EARLY = 5


def row_of(dz, dx):
    return PLACE[dz] * GROUP + dx * ROWS


def pack_of(dz, dx):
    return (dz * NX + dx) * PACK


def plan():
    msgs, tasks = {}, []

    first_sends, hold = [], []
    by_dz = {dz: [] for dz in range(NZ)}
    for kind, f, g, cols in (("A", "x", "z", CA), ("B", "z", "x", CB)):
        for tw in (0, 1):
            def at(cf, cg):
                dx, dz = (cf, cg) if f == "x" else (cg, cf)
                return dz % NZ, dx % NX

            def send(cf, cg, axis, up):
                step = -1 if up else 1
                nf, ng = (cf + step, cg) if axis == f else (cf, cg + step)
                dst = at(nf, ng)
                link = axis + ("+" if up else "-")
                keys = []
                for what, name, size in (("G", "ag", ROWS * cols), ("E", "age", PACK * cols // 2)):
                    key = (name, kind, tw) + dst
                    msgs[key] = Msg(link, size * 2, (what, kind, tw) + at(cf, cg), (what, kind, tw) + dst)
                    keys.append(key)
                by_dz[dst[0]].extend(keys)
                return keys

            def visit(cf, cg, via, up, hops):
                out = []
                if via in (None, f):
                    for u in (True, False):
                        reach = REACH[tw][f][0 if u else 1]
                        if via is None or (u == up and hops < reach):
                            out.append((send(cf, cg, f, u), cf + (-1 if u else 1), cg, f, u, 1 if via is None else hops + 1))
                    for u in (True, False):
                        out.append((send(cf, cg, g, u), cf, cg + (-1 if u else 1), g, u, 1))
                elif hops < REACH[tw][g][0 if up else 1]:
                    out.append((send(cf, cg, g, up), cf, cg + (-1 if up else 1), g, up, hops + 1))
                if via is None:
                    first_sends.extend(k for o in out for k in o[0])
                elif out:
                    here = (kind, tw) + at(cf, cg)
                    sends = [k for o in out for k in o[0]]
                    tasks.append(Task(("fwd",) + here, [("ag",) + here, ("age",) + here], sends, 0.05, 0))
                    if any(msgs[k].link[0] == "x" for k in sends):
                        hold.append(("fwd",) + here)
                for key, a, b, v, u, h in out:
                    visit(a, b, v, u, h)

            visit(0, 0, None, None, 0)
    tasks.append(Task("pick", [], first_sends, 2.0, 0, ("pick",)))

    for dz in range(NZ):
        tasks.append(Task(("main", dz), ["pick", "weights"] + by_dz[dz], [], 3.0, 3, ("main", dz)))
    tasks.append(Task("weights", ["pick"], [], 0.1, 1, ("weights",)))
    task_of = {t.name: t for t in tasks}

    def chain(kind, tw, axis, up, fixed, at_of, blocks, ready, packed=False):
        c0, cols = RS_COLS[kind, tw]
        what, nrows = "P", ROWS * blocks
        if packed:
            what, nrows, c0, cols = "P" + kind, PACK * blocks, 0, (CA if kind == "A" else CB) // 2
        reach = REACH[tw][axis][0 if up else 1]
        sign = 1 if up else -1
        prev = None
        for k in range(reach, -1, -1):
            here = (sign * k) % SIZE[axis]
            r0 = pack_of(*at_of(here)) if packed else row_of(*at_of(here))
            name = ("rs", kind, tw, axis, up, fixed, packed, k)
            key = ("rsm", kind, tw, axis, up, fixed, packed, k - 1)
            deps = list(ready(here))
            if prev is not None:
                deps.append(prev)
            sends = []
            if k > 0:
                msgs[key] = Msg(
                    axis + ("+" if up else "-"), nrows * cols * 2, (what, r0, nrows, c0, cols), ("R", key, nrows, cols)
                )
                sends = [key]
            emit = None if prev is None else ("add", prev, what, r0, nrows, c0, cols)
            dur = 0.0 if prev is None else 0.1 + nrows * cols * 2 / 1.5e6
            tasks.append(Task(name, deps, sends, dur, 1 if k else 2, emit))
            prev = key
        return name

    later = {dz: [("main", 4)] if dz in (0, 1, 7) else [] for dz in range(NZ)}
    ends = []
    for tw, packed in ((0, False), (1, False), (0, True), (1, True)):
        if not (packed and tw == 1):
            za = {
                p: [
                    chain("A", tw, "z", up, p, lambda h, p=p: (h, p), 2, lambda h: [("main", h)], packed)
                    for up in (True, False)
                ]
                for p in (2, 0)
            }
            ends += [
                chain("A", tw, "x", up, 0, lambda h: (0, h), 1, lambda h: za[h // 2 * 2], packed)
                for up in (True, False)
            ]
        if packed and tw == 0:
            continue
        xb = {}
        for dz in (4, 3, 5, 2, 6, 1, 7, 0):
            xb[dz] = [
                chain(
                    "B", tw, "x", up, dz, lambda h, dz=dz: (dz, h), 1, lambda h, dz=dz: [("main", dz)] + hold + later[dz], packed
                )
                for up in (True, False)
            ]
        ends += [
            chain("B", tw, "z", up, 0, lambda h: (h, 0), 1, lambda h: xb[h], packed)
            for up in (True, False)
        ]
    tasks.append(Task("final", ends, [], 1.5, 5, ("final",)))

    mains = [("main", dz) for dz in range(NZ)]
    tasks.append(Task("turn early", [("main", dz) for dz in PLACE if PLACE[dz] < EARLY], [], 1.0, 4, ("turn", 0)))
    early = "turn early"
    for u, (r0, nrows) in enumerate(UNITS):
        for kind, count in (("A", CA // 256), ("B", CB // 256)):
            for i in range(count):
                tasks.append(Task(("early", u, kind, i), [early], [], 0.1 + nrows / 1200, 4, ("early", u, kind, i)))
                early = tasks[-1].name
    tasks.append(Task("turn", mains + [early], [], 0.7, 4, ("turn", 1)))
    last, dp_ends = "turn", []
    for u, (r0, nrows) in enumerate(UNITS):
        for kind, count in (("A", CA // 256), ("B", CB // 256)):
            for i in range(count):
                tasks.append(Task(("grad", u, kind, i), [last], [], 0.1 + nrows / 1500, 4, ("grad", u, kind, i)))
                last = tasks[-1].name
        for dy in (2, 3, 1, 0):
            msgs["cx", u, dy] = Msg("core", nrows * SH * 2, ("W", dy, True, r0, nrows), ("CX", dy, r0, nrows))
            tasks[-1].sends.append(("cx", u, dy))
        for dy in (2, 3, 1, 0):
            tasks.append(Task(("cadd", u, dy), [last, ("cx", u, dy)], [], 0.1 + nrows / 1500, 2, ("cadd", dy, r0, nrows)))
        half = nrows // 2
        for tw in (0, 1):
            for up in (True, False):
                reach = REACH[tw]["x"][0 if up else 1]
                prev = None
                for k in range(reach, -1, -1):
                    dy = (k if up else -k) % NY
                    name = ("y", u, tw, up, k)
                    key = ("ym", u, tw, up, k - 1)
                    place = (dy, r0 + tw * half, half)
                    deps = [("cadd", u, dy)] + ([prev] if prev else [])
                    sends = []
                    if k > 0:
                        msgs[key] = Msg(
                            "y" + ("+" if up else "-"), half * SH * 2, ("W", dy, False) + place[1:], ("Y", key)
                        )
                        sends = [key]
                    emit = None if prev is None else ("yadd", prev) + place
                    tasks.append(Task(name, deps, sends, 0.0 if prev is None else 0.1 + half / 1500, 2, emit))
                    prev = key
                dp_ends.append(name)
    tasks.append(Task("wout", dp_ends, [], 0.3, 5, ("wout",)))
    return msgs, schedule(msgs, tasks)


def schedule(msgs, tasks):
    waiting = {i: set(t.deps) for i, t in enumerate(tasks)}
    users = {}
    for i, t in enumerate(tasks):
        for d in t.deps:
            users.setdefault(d, []).append(i)
    tail = {}

    def tail_of(key):
        if key not in tail:
            tail[key] = 0.0
            for i in users.get(key, ()):
                t = tasks[i]
                sent = max([msgs[k].size / LINK_RATE + LATENCY + tail_of(k) for k in t.sends], default=0.0)
                tail[key] = max(tail[key], t.dur + max(sent, tail_of(t.name)))
        return tail[key]

    for t in tasks:
        sent = max([msgs[k].size / LINK_RATE + LATENCY + tail_of(k) for k in t.sends], default=0.0)
        t.tail = max(sent, tail_of(t.name))
    ready, arrivals, free, now, order = [], [], {}, 0.0, []
    times = {}

    def satisfy(key):
        for i in users.get(key, ()):
            waiting[i].discard(key)
            if not waiting[i]:
                heapq.heappush(ready, (tasks[i].rank, -tasks[i].tail, i))

    for i in range(len(tasks)):
        if not waiting[i]:
            heapq.heappush(ready, (tasks[i].rank, -tasks[i].tail, i))
    seq = 0
    while ready or arrivals:
        while arrivals and arrivals[0][0] <= now:
            satisfy(heapq.heappop(arrivals)[2])
        if not ready:
            now = arrivals[0][0]
            continue
        i = heapq.heappop(ready)[2]
        t = tasks[i]
        now += t.dur
        order.append(t)
        times[t.name] = now
        for key in t.sends:
            m = msgs[key]
            start = max(now, free.get(m.link, 0.0))
            rate = CORE_RATE if m.link == "core" else LINK_RATE
            free[m.link] = start + m.size / rate
            seq += 1
            heapq.heappush(arrivals, (free[m.link] + LATENCY, seq, key))
        satisfy(t.name)
    if len(order) != len(tasks):
        raise ValueError("stuck")
    plan.times, plan.end = times, now
    return order


MSGS, ORDER = plan()
KEYS = sorted(MSGS, key=repr)
INDEX = {k: i for i, k in enumerate(KEYS)}
R_SLOT, R_COUNT = {}, {}
for _k in KEYS:
    if _k[0] == "rsm":
        _, _, _nr, _nc = MSGS[_k].dst
        R_SLOT[_k] = R_COUNT.get((_nr, _nc), 0)
        R_COUNT[_nr, _nc] = R_SLOT[_k] + 1
R_SHAPES = sorted(R_COUNT)
Y_SLOT = {}
for _k in KEYS:
    if _k[0] == "ym":
        Y_SLOT[_k] = sum(o[1] == _k[1] for o in Y_SLOT)


def kernel(ids, probs, tokens, cot, wg_hbm, wu_hbm, wd_hbm, ret_out, across_out, g_out, u_out, d_out,
           ga0, ga1, gb0, gb1, ea0, ea1, eb0, eb1, part, pa, pb, wg, wu, wd, gback, uback, hid, turned0, turned1, acc, w3, cx, yr0, yr1, *rest):
    landing = dict(zip(R_SHAPES, rest[: len(R_SHAPES)]))
    wsem, send_sem, recv_sem = rest[len(R_SHAPES):]
    gathered = {("A", 0): ga0, ("A", 1): ga1, ("B", 0): gb0, ("B", 1): gb1}
    extras = {("A", 0): ea0, ("A", 1): ea1, ("B", 0): eb0, ("B", 1): eb1}
    yr = (yr0, yr1)
    sums = {"P": part, "PA": pa, "PB": pb}

    e = lax.axis_index("expert")
    d = lax.axis_index("dp")
    x, z, y, c = e // NZ, e % NZ, d // 2, d % 2
    peer = {
        "z+": {"expert": x * NZ + (z + 1) % NZ},
        "z-": {"expert": x * NZ + (z + NZ - 1) % NZ},
        "x+": {"expert": ((x + 1) % NX) * NZ + z},
        "x-": {"expert": ((x + NX - 1) % NX) * NZ + z},
        "y+": {"dp": ((y + 1) % NY) * 2 + c},
        "y-": {"dp": ((y + NY - 1) % NY) * 2 + c},
        "core": {"dp": y * 2 + 1 - c},
    }
    loads = [
        pltpu.make_async_copy(src, dst, wsem.at[i])
        for i, (src, dst) in enumerate(((wg_hbm, wg), (wu_hbm, wu), (wd_hbm, wd)))
    ]
    for load in loads:
        load.start()
    barrier = pltpu.get_barrier_semaphore()
    for target in peer.values():
        pl.semaphore_signal(barrier, inc=1, device_id=target, device_id_type=pl.DeviceIdType.MESH)

    def shard(dy, other):
        owner = ((y + dy) % NY) * 2 + (1 - c if other else c)
        return pl.ds(pl.multiple_of(owner * SH, 128), SH)

    def ref_of(place):
        what = place[0]
        if what == "G":
            _, kind, tw, dz, dx = place
            return gathered[kind, tw].at[pl.ds(row_of(dz, dx), ROWS), :]
        if what == "E":
            _, kind, tw, dz, dx = place
            return extras[kind, tw].at[pl.ds(pack_of(dz, dx), PACK), :]
        if what in sums:
            _, r0, nr, c0, nc = place
            return sums[what].at[pl.ds(r0, nr), pl.ds(c0, nc)]
        if what == "R":
            _, key, nr, nc = place
            return landing[nr, nc].at[R_SLOT[key]]
        if what == "W":
            _, dy, other, r0, nr = place
            return w3.at[pl.ds(r0, nr), shard(dy, other)]
        if what == "CX":
            _, dy, r0, nr = place
            return cx.at[dy, pl.ds(r0, nr), :]
        return yr[place[1][1]].at[Y_SLOT[place[1]]]

    copies = {}

    def copy_of(key):
        if key not in copies:
            m = MSGS[key]
            copies[key] = pltpu.make_async_remote_copy(
                src_ref=ref_of(m.src),
                dst_ref=ref_of(m.dst),
                send_sem=send_sem.at[INDEX[key]],
                recv_sem=recv_sem.at[INDEX[key]],
                device_id=peer[m.link],
                device_id_type=pl.DeviceIdType.MESH,
            )
        return copies[key]

    def pick():
        hits = ids[...] == 0
        chosen = jnp.sum(jnp.where(hits, 1.0, 0.0), axis=0, keepdims=True)
        share = jnp.sum(jnp.where(hits, probs[...], 0.0), axis=0, keepdims=True)
        above = lax.broadcasted_iota(jnp.int32, (TOK, TOK), 0) < lax.broadcasted_iota(jnp.int32, (TOK, TOK), 1)
        wide = jnp.broadcast_to(chosen, (TOK, TOK))
        slot = jnp.dot(
            wide.astype(BF), jnp.where(above, 1.0, 0.0).astype(BF), preferred_element_type=F32
        )
        row = lax.broadcasted_iota(jnp.int32, (TOK, TOK), 0).astype(F32)
        whole = jnp.where((slot == row) & (wide > 0.5), 1.0, 0.0)
        across_out[...] = whole[: ROWS + PACK].astype(BF)
        low = whole[ROWS : ROWS + PACK]
        r8 = lax.broadcasted_iota(jnp.int32, (PACK, TOK), 0)
        wanted = (r8 + (ROWS - EXTRA)).astype(F32)
        high = jnp.where((slot[:PACK] == wanted) & (wide[:PACK] > 0.5) & (r8 >= EXTRA), 1.0, 0.0)
        maps = [whole[:ROWS], low, high]
        shares = [jnp.sum(m * share, axis=1, keepdims=True) for m in maps]
        maps = [m.astype(BF) for m in maps]

        def take(k, source, c0, cols, scale):
            got = jnp.dot(maps[k], source[:, pl.ds(c0, cols)], preferred_element_type=F32)
            return got * shares[k] if scale else got

        for c0, cols, kind in ((0, CA, "A"), (CA, CB, "B")):
            for tw, source in ((0, tokens), (1, cot)):
                gathered[kind, tw][pl.ds(0, ROWS), :] = take(0, source, c0, cols, tw == 1).astype(BF)
                extras[kind, tw][pl.ds(0, PACK), :] = (
                    take(1, source, c0, cols // 2, tw == 1) + take(2, source, c0 + cols // 2, cols // 2, tw == 1)
                ).astype(BF)
        pl.semaphore_wait(barrier, len(peer))

    def spread(high, shape, axis):
        i = lax.broadcasted_iota(jnp.int32, shape, axis)
        j = lax.broadcasted_iota(jnp.int32, shape, 1 - axis)
        return jnp.where((i >> 2) * PACK + (i & 3) + (EXTRA if high else 0) == j, 1.0, 0.0).astype(BF)

    def weights():
        for load in loads:
            load.wait()

    nt = (((1,), (1,)), ((), ()))

    def main(dz):
        rows = pl.ds(row_of(dz, 0), GROUP)
        tail = pl.ds(row_of(dz, 0) + NX * ROWS, NX * EXTRA)
        packed = pl.ds(pack_of(dz, 0), NX * PACK)
        for kind, cols in (("A", CA // 2), ("B", CB // 2)):
            for tw in (0, 1):
                for high in (0, 1):
                    gathered[kind, tw][tail, pl.ds(high * cols, cols)] = jnp.dot(
                        spread(high, (NX * EXTRA, NX * PACK), 0), extras[kind, tw][packed, :],
                        preferred_element_type=F32,
                    ).astype(BF)
        ra, rb, sa, sb = ga0[rows, :], gb0[rows, :], ga1[rows, :], gb1[rows, :]
        gate = jnp.dot(ra, wg[pl.ds(0, CA), :], preferred_element_type=F32) + jnp.dot(
            rb, wg[pl.ds(CA, CB), :], preferred_element_type=F32
        )
        up = jnp.dot(ra, wu[pl.ds(0, CA), :], preferred_element_type=F32) + jnp.dot(
            rb, wu[pl.ds(CA, CB), :], preferred_element_type=F32
        )
        back = lax.dot_general(sa, wd[:, pl.ds(0, CA)], nt, preferred_element_type=F32) + lax.dot_general(
            sb, wd[:, pl.ds(CA, CB)], nt, preferred_element_type=F32
        )
        sigma = jax.nn.sigmoid(gate)
        act = gate * sigma
        hid[rows, :] = (act * up).astype(BF)
        gb = (back * up * sigma * (1.0 + gate * (1.0 - sigma))).astype(BF)
        ub = (back * act).astype(BF)
        gback[rows, :] = gb
        uback[rows, :] = ub
        for c0 in range(0, D, 256):
            cols = pl.ds(c0, 256)
            part[rows, cols] = (
                lax.dot_general(gb, wg[cols, :], nt, preferred_element_type=F32)
                + lax.dot_general(ub, wu[cols, :], nt, preferred_element_type=F32)
            ).astype(BF)

        for out, c0, cols in ((pa, 0, CA // 2), (pb, CA, CB // 2)):
            out[packed, :] = sum(
                jnp.dot(
                    spread(high, (NX * PACK, NX * EXTRA), 1), part[tail, pl.ds(c0 + high * cols, cols)],
                    preferred_element_type=F32,
                )
                for high in (0, 1)
            ).astype(BF)

    def add(key, what, r0, nr, c0, nc):
        got = landing[nr, nc].at[R_SLOT[key]]
        here = (pl.ds(r0, nr), pl.ds(c0, nc))
        sums[what][here] = sums[what][here] + got[...]

    cut = EARLY * GROUP
    halves = ((0, cut), (cut, NZ * GROUP - cut))

    def turn(late):
        rows = pl.ds(*halves[late])
        for i, source in enumerate((gback, uback, hid)):
            (turned1 if late else turned0)[pl.ds(i * H, H), :] = jnp.transpose(source[rows, :])

    def product(u, kind, i, late):
        return jnp.dot(
            (turned1 if late else turned0)[pl.ds(*UNITS[u]), :],
            gathered[kind, u][pl.ds(*halves[late]), pl.ds(i * 256, 256)],
            preferred_element_type=F32,
        )

    def tile(u, kind, i):
        return pl.ds(*UNITS[u]), pl.ds((0 if kind == "A" else CA) + i * 256, 256)

    def early(u, kind, i):
        acc[tile(u, kind, i)] = product(u, kind, i, 0)

    def grad(u, kind, i):
        here = tile(u, kind, i)
        w3[here] = (acc[here] + product(u, kind, i, 1)).astype(BF)

    def cadd(dy, r0, nr):
        here = (pl.ds(r0, nr), shard(dy, False))
        w3[here] = w3[here] + cx[dy, pl.ds(r0, nr), :]

    def yadd(key, dy, r0, nr):
        here = (pl.ds(r0, nr), shard(dy, False))
        w3[here] = w3[here] + yr[key[1]][Y_SLOT[key]]

    def final():
        ret_out[pl.ds(0, ROWS), :] = part[pl.ds(0, ROWS), :]
        for packed, c0, cols in ((pa, 0, CA // 2), (pb, CA, CB // 2)):
            for high in (0, 1):
                ret_out[pl.ds(ROWS, PACK), pl.ds(c0 + high * cols, cols)] = jnp.dot(
                    spread(high, (PACK, NX * PACK), 0), packed[pl.ds(0, NX * PACK), :],
                    preferred_element_type=F32,
                ).astype(BF)

    def wout():
        own = shard(0, False)
        for i, out in enumerate((g_out, u_out, d_out)):
            out[...] = w3[pl.ds(i * H, H), own]

    run = dict(early=early, pick=pick, weights=weights, main=main, add=add, turn=turn, grad=grad,
               cadd=cadd, yadd=yadd, final=final, wout=wout)
    arrived = set()
    for task in ORDER:
        for dep in task.deps:
            if dep in MSGS and dep not in arrived:
                copy_of(dep).wait_recv()
                arrived.add(dep)
        if task.emit is not None:
            run[task.emit[0]](*task.emit[1:])
        for key in task.sends:
            copy_of(key).start()
    for key in KEYS:
        copy_of(key).wait_send()


def per_device(tokens, cotangent, route_ids, route_probs, gate_weight, up_weight, down_weight):
    vmem = pl.BlockSpec(memory_space=pltpu.VMEM)
    anywhere = pl.BlockSpec(memory_space=pl.ANY)
    rows, packs = NZ * GROUP, NZ * NX * PACK
    scratch = [
        pltpu.VMEM((rows, CA), BF), pltpu.VMEM((rows, CA), BF),
        pltpu.VMEM((rows, CB), BF), pltpu.VMEM((rows, CB), BF),
        pltpu.VMEM((packs, CA // 2), BF), pltpu.VMEM((packs, CA // 2), BF),
        pltpu.VMEM((packs, CB // 2), BF), pltpu.VMEM((packs, CB // 2), BF),
        pltpu.VMEM((rows, D), BF),
        pltpu.VMEM((packs, CA // 2), BF), pltpu.VMEM((packs, CB // 2), BF),
        pltpu.VMEM((D, H), BF), pltpu.VMEM((D, H), BF), pltpu.VMEM((H, D), BF),
        pltpu.VMEM((rows, H), BF), pltpu.VMEM((rows, H), BF), pltpu.VMEM((rows, H), BF),
        pltpu.VMEM((3 * H, EARLY * GROUP), BF), pltpu.VMEM((3 * H, rows - EARLY * GROUP), BF),
        pltpu.VMEM((3 * H, D), F32),
        pltpu.VMEM((3 * H, D), BF),
        pltpu.VMEM((NY, 3 * H, SH), BF),
        *(pltpu.VMEM((len(Y_SLOT) // 2, nrows // 2, SH), BF) for _, nrows in UNITS),
    ]
    scratch += [pltpu.VMEM((R_COUNT[s],) + s, BF) for s in R_SHAPES]
    scratch += [
        pltpu.SemaphoreType.DMA((3,)),
        pltpu.SemaphoreType.DMA((len(KEYS),)),
        pltpu.SemaphoreType.DMA((len(KEYS),)),
    ]
    returned, across, gate_grad, up_grad, down_grad = pl.pallas_call(
        kernel,
        out_shape=(
            jax.ShapeDtypeStruct((ROWS + PACK, D), BF),
            jax.ShapeDtypeStruct((ROWS + PACK, TOK), BF),
            *(jax.ShapeDtypeStruct((H, SH), BF) for _ in range(3)),
        ),
        in_specs=[vmem, vmem, vmem, vmem, anywhere, anywhere, anywhere],
        out_specs=(vmem,) * 5,
        scratch_shapes=scratch,
        compiler_params=pltpu.CompilerParams(
            collective_id=0, has_side_effects=True, vmem_limit_bytes=67043328
        ),
    )(route_ids.T, route_probs.T, tokens, cotangent, gate_weight, up_weight, down_weight)
    token_grad = lax.dot_general(
        across, returned, (((0,), (0,)), ((), ())), preferred_element_type=F32
    ).astype(BF)
    return token_grad, gate_grad.T, up_grad.T, down_grad


def solution(mesh):
    in_specs = (
        P(("dp", "expert"), None),
        P(("dp", "expert"), None),
        P(("dp", "expert"), None),
        P(("dp", "expert"), None),
        P(None, "expert"),
        P(None, "expert"),
        P("expert", None),
    )
    out_specs = (P(("dp", "expert"), None), P("dp", "expert"), P("dp", "expert"), P("expert", "dp"))
    return jax.shard_map(
        per_device, mesh=mesh, in_specs=in_specs, out_specs=out_specs, check_vma=False
    )
```

```python
import functools
import heapq

import jax
import jax.numpy as jnp
from jax import lax
from jax.experimental import pallas as pl
from jax.experimental.pallas import tpu as pltpu
from jax.sharding import PartitionSpec as P

CAP = 36
ROWS = 32
PACK = 8
EXTRA = CAP - ROWS
TOK = 128
D = 3072
H = 256
CA = 1280
CB = D - CA
NX, NZ, NY = 4, 8, 4
SH = D // 8
UNITS = ((0, 2 * H), (2 * H, H))
BF = jnp.bfloat16
F32 = jnp.float32
LINK_RATE = 46e3
CORE_RATE = 250e3
LATENCY = 1.6

REACH = {
    0: {"x": (2, 1), "z": (4, 3)},
    1: {"x": (1, 2), "z": (3, 4)},
}
SIZE = {"x": NX, "z": NZ, "y": NY}
RS_COLS = {
    ("A", 0): (0, CA // 2),
    ("A", 1): (CA // 2, CA // 2),
    ("B", 0): (CA, CB // 2),
    ("B", 1): (CA + CB // 2, CB // 2),
}


class Msg:
    def __init__(self, link, size, src, dst):
        self.link, self.size, self.src, self.dst = link, size, src, dst


class Task:
    def __init__(self, name, deps, sends=(), dur=0.0, rank=0, emit=None):
        self.name, self.deps, self.sends = name, tuple(deps), list(sends)
        self.dur, self.rank, self.emit = dur, rank, emit


GROUP = NX * CAP


PLACE = {dz: i for i, dz in enumerate((0, 1, 7, 2, 6, 3, 5, 4))}
EARLY = 5
BATCHES = ((0,), (1, 7), (2, 6), (3, 5), (4,))


def row_of(dz, dx):
    return PLACE[dz] * GROUP + dx * ROWS


def pack_of(dz, dx):
    return (dz * NX + dx) * PACK


def plan():
    msgs, tasks = {}, []

    first_sends, hold = [], []
    by_dz = {dz: [] for dz in range(NZ)}
    for kind, f, g, cols in (("A", "x", "z", CA), ("B", "z", "x", CB)):
        for tw in (0, 1):
            def at(cf, cg):
                dx, dz = (cf, cg) if f == "x" else (cg, cf)
                return dz % NZ, dx % NX

            def send(cf, cg, axis, up):
                step = -1 if up else 1
                nf, ng = (cf + step, cg) if axis == f else (cf, cg + step)
                dst = at(nf, ng)
                link = axis + ("+" if up else "-")
                keys = []
                for what, name, size in (("G", "ag", ROWS * cols), ("E", "age", PACK * cols // 2)):
                    key = (name, kind, tw) + dst
                    msgs[key] = Msg(link, size * 2, (what, kind, tw) + at(cf, cg), (what, kind, tw) + dst)
                    keys.append(key)
                by_dz[dst[0]].extend(keys)
                return keys

            def visit(cf, cg, via, up, hops):
                out = []
                if via in (None, f):
                    for u in (True, False):
                        reach = REACH[tw][f][0 if u else 1]
                        if via is None or (u == up and hops < reach):
                            out.append((send(cf, cg, f, u), cf + (-1 if u else 1), cg, f, u, 1 if via is None else hops + 1))
                    for u in (True, False):
                        out.append((send(cf, cg, g, u), cf, cg + (-1 if u else 1), g, u, 1))
                elif hops < REACH[tw][g][0 if up else 1]:
                    out.append((send(cf, cg, g, up), cf, cg + (-1 if up else 1), g, up, hops + 1))
                if via is None:
                    first_sends.extend(k for o in out for k in o[0])
                elif out:
                    here = (kind, tw) + at(cf, cg)
                    sends = [k for o in out for k in o[0]]
                    tasks.append(Task(("fwd",) + here, [("ag",) + here, ("age",) + here], sends, 0.05, 0))
                    if any(msgs[k].link[0] == "x" for k in sends):
                        hold.append(("fwd",) + here)
                for key, a, b, v, u, h in out:
                    visit(a, b, v, u, h)

            visit(0, 0, None, None, 0)
    tasks.append(Task("pick", [], first_sends, 2.0, 0, ("pick",)))

    for group in BATCHES:
        deps = ["pick", "weights"] + [k for dz in group for k in by_dz[dz]]
        dur = 2.5 + 2.0 * len(group)
        tasks.append(Task(("main", group[0]), deps, [], dur, 3, ("main",) + group))
        for dz in group[1:]:
            tasks.append(Task(("main", dz), [("main", group[0])], [], 0.0, 1))
    tasks.append(Task("weights", ["pick"], [], 0.1, 1, ("weights",)))
    task_of = {t.name: t for t in tasks}

    def chain(kind, tw, axis, up, fixed, at_of, blocks, ready, packed=False):
        c0, cols = RS_COLS[kind, tw]
        what, nrows = "P", ROWS * blocks
        if packed:
            what, nrows, c0, cols = "P" + kind, PACK * blocks, 0, (CA if kind == "A" else CB) // 2
        reach = REACH[tw][axis][0 if up else 1]
        sign = 1 if up else -1
        prev = None
        for k in range(reach, -1, -1):
            here = (sign * k) % SIZE[axis]
            r0 = pack_of(*at_of(here)) if packed else row_of(*at_of(here))
            name = ("rs", kind, tw, axis, up, fixed, packed, k)
            key = ("rsm", kind, tw, axis, up, fixed, packed, k - 1)
            deps = list(ready(here))
            if prev is not None:
                deps.append(prev)
            sends = []
            if k > 0:
                msgs[key] = Msg(
                    axis + ("+" if up else "-"), nrows * cols * 2, (what, r0, nrows, c0, cols), ("R", key, nrows, cols)
                )
                sends = [key]
            emit = None if prev is None else ("add", prev, what, r0, nrows, c0, cols)
            dur = 0.0 if prev is None else 0.1 + nrows * cols * 2 / 1.5e6
            tasks.append(Task(name, deps, sends, dur, 1 if k else 2, emit))
            prev = key
        return name

    later = {dz: [("main", 4)] if dz in (0, 1, 7) else [] for dz in range(NZ)}
    ends = []
    for tw, packed in ((0, False), (1, False), (0, True), (1, True)):
        if not (packed and tw == 1):
            za = {
                p: [
                    chain("A", tw, "z", up, p, lambda h, p=p: (h, p), 2, lambda h: [("main", h)], packed)
                    for up in (True, False)
                ]
                for p in (2, 0)
            }
            ends += [
                chain("A", tw, "x", up, 0, lambda h: (0, h), 1, lambda h: za[h // 2 * 2], packed)
                for up in (True, False)
            ]
        if packed and tw == 0:
            continue
        xb = {}
        for dz in (4, 3, 5, 2, 6, 1, 7, 0):
            xb[dz] = [
                chain(
                    "B", tw, "x", up, dz, lambda h, dz=dz: (dz, h), 1, lambda h, dz=dz: [("main", dz)] + hold + later[dz], packed
                )
                for up in (True, False)
            ]
        ends += [
            chain("B", tw, "z", up, 0, lambda h: (h, 0), 1, lambda h: xb[h], packed)
            for up in (True, False)
        ]
    tasks.append(Task("final", ends, [], 1.5, 5, ("final",)))

    mains = [("main", dz) for dz in range(NZ)]
    tasks.append(Task("turn early", [("main", dz) for dz in PLACE if PLACE[dz] < EARLY], [], 1.0, 4, ("turn", 0)))
    early = "turn early"
    for u, (r0, nrows) in enumerate(UNITS):
        for kind, count in (("A", CA // 256), ("B", CB // 256)):
            for i in range(count):
                tasks.append(Task(("early", u, kind, i), [early], [], 0.1 + nrows / 1200, 4, ("early", u, kind, i)))
                early = tasks[-1].name
    tasks.append(Task("turn", mains + [early], [], 0.7, 4, ("turn", 1)))
    last, dp_ends = "turn", []
    for u, (r0, nrows) in enumerate(UNITS):
        for kind, count in (("A", CA // 256), ("B", CB // 256)):
            for i in range(count):
                tasks.append(Task(("grad", u, kind, i), [last], [], 0.1 + nrows / 1500, 4, ("grad", u, kind, i)))
                last = tasks[-1].name
        for dy in (2, 3, 1, 0):
            msgs["cx", u, dy] = Msg("core", nrows * SH * 2, ("W", dy, True, r0, nrows), ("CX", dy, r0, nrows))
            tasks[-1].sends.append(("cx", u, dy))
        for dy in (2, 3, 1, 0):
            tasks.append(Task(("cadd", u, dy), [last, ("cx", u, dy)], [], 0.1 + nrows / 1500, 2, ("cadd", dy, r0, nrows)))
        half = nrows // 2
        for tw in (0, 1):
            for up in (True, False):
                reach = REACH[tw]["x"][0 if up else 1]
                prev = None
                for k in range(reach, -1, -1):
                    dy = (k if up else -k) % NY
                    name = ("y", u, tw, up, k)
                    key = ("ym", u, tw, up, k - 1)
                    place = (dy, r0 + tw * half, half)
                    deps = [("cadd", u, dy)] + ([prev] if prev else [])
                    sends = []
                    if k > 0:
                        msgs[key] = Msg(
                            "y" + ("+" if up else "-"), half * SH * 2, ("W", dy, False) + place[1:], ("Y", key)
                        )
                        sends = [key]
                    emit = None if prev is None else ("yadd", prev) + place
                    tasks.append(Task(name, deps, sends, 0.0 if prev is None else 0.1 + half / 1500, 2, emit))
                    prev = key
                dp_ends.append(name)
    tasks.append(Task("wout", dp_ends, [], 0.3, 5, ("wout",)))
    return msgs, schedule(msgs, tasks)


def schedule(msgs, tasks):
    waiting = {i: set(t.deps) for i, t in enumerate(tasks)}
    users = {}
    for i, t in enumerate(tasks):
        for d in t.deps:
            users.setdefault(d, []).append(i)
    tail = {}

    def tail_of(key):
        if key not in tail:
            tail[key] = 0.0
            for i in users.get(key, ()):
                t = tasks[i]
                sent = max([msgs[k].size / LINK_RATE + LATENCY + tail_of(k) for k in t.sends], default=0.0)
                tail[key] = max(tail[key], t.dur + max(sent, tail_of(t.name)))
        return tail[key]

    for t in tasks:
        sent = max([msgs[k].size / LINK_RATE + LATENCY + tail_of(k) for k in t.sends], default=0.0)
        t.tail = max(sent, tail_of(t.name))
    ready, arrivals, free, now, order = [], [], {}, 0.0, []
    times = {}

    def satisfy(key):
        for i in users.get(key, ()):
            waiting[i].discard(key)
            if not waiting[i]:
                heapq.heappush(ready, (tasks[i].rank, -tasks[i].tail, i))

    for i in range(len(tasks)):
        if not waiting[i]:
            heapq.heappush(ready, (tasks[i].rank, -tasks[i].tail, i))
    seq = 0
    while ready or arrivals:
        while arrivals and arrivals[0][0] <= now:
            satisfy(heapq.heappop(arrivals)[2])
        if not ready:
            now = arrivals[0][0]
            continue
        i = heapq.heappop(ready)[2]
        t = tasks[i]
        now += t.dur
        order.append(t)
        times[t.name] = now
        for key in t.sends:
            m = msgs[key]
            start = max(now, free.get(m.link, 0.0))
            rate = CORE_RATE if m.link == "core" else LINK_RATE
            free[m.link] = start + m.size / rate
            seq += 1
            heapq.heappush(arrivals, (free[m.link] + LATENCY, seq, key))
        satisfy(t.name)
    if len(order) != len(tasks):
        raise ValueError("stuck")
    plan.times, plan.end = times, now
    return order


MSGS, ORDER = plan()
KEYS = sorted(MSGS, key=repr)
INDEX = {k: i for i, k in enumerate(KEYS)}
R_SLOT, R_COUNT = {}, {}
for _k in KEYS:
    if _k[0] == "rsm":
        _, _, _nr, _nc = MSGS[_k].dst
        R_SLOT[_k] = R_COUNT.get((_nr, _nc), 0)
        R_COUNT[_nr, _nc] = R_SLOT[_k] + 1
R_SHAPES = sorted(R_COUNT)
Y_SLOT = {}
for _k in KEYS:
    if _k[0] == "ym":
        Y_SLOT[_k] = sum(o[1] == _k[1] for o in Y_SLOT)


def kernel(ids, probs, tokens, cot, wg_hbm, wu_hbm, wd_hbm, ret_out, across_out, g_out, u_out, d_out,
           ga0, ga1, gb0, gb1, ea0, ea1, eb0, eb1, part, pa, pb, wg, wu, wd, gback, uback, hid, turned0, turned1, acc, w3, cx, yr0, yr1, *rest):
    landing = dict(zip(R_SHAPES, rest[: len(R_SHAPES)]))
    wsem, send_sem, recv_sem = rest[len(R_SHAPES):]
    gathered = {("A", 0): ga0, ("A", 1): ga1, ("B", 0): gb0, ("B", 1): gb1}
    extras = {("A", 0): ea0, ("A", 1): ea1, ("B", 0): eb0, ("B", 1): eb1}
    yr = (yr0, yr1)
    sums = {"P": part, "PA": pa, "PB": pb}

    e = lax.axis_index("expert")
    d = lax.axis_index("dp")
    x, z, y, c = e // NZ, e % NZ, d // 2, d % 2
    peer = {
        "z+": {"expert": x * NZ + (z + 1) % NZ},
        "z-": {"expert": x * NZ + (z + NZ - 1) % NZ},
        "x+": {"expert": ((x + 1) % NX) * NZ + z},
        "x-": {"expert": ((x + NX - 1) % NX) * NZ + z},
        "y+": {"dp": ((y + 1) % NY) * 2 + c},
        "y-": {"dp": ((y + NY - 1) % NY) * 2 + c},
        "core": {"dp": y * 2 + 1 - c},
    }
    loads = [
        pltpu.make_async_copy(src, dst, wsem.at[i])
        for i, (src, dst) in enumerate(((wg_hbm, wg), (wu_hbm, wu), (wd_hbm, wd)))
    ]
    for load in loads:
        load.start()
    barrier = pltpu.get_barrier_semaphore()
    for target in peer.values():
        pl.semaphore_signal(barrier, inc=1, device_id=target, device_id_type=pl.DeviceIdType.MESH)

    def shard(dy, other):
        owner = ((y + dy) % NY) * 2 + (1 - c if other else c)
        return pl.ds(pl.multiple_of(owner * SH, 128), SH)

    def ref_of(place):
        what = place[0]
        if what == "G":
            _, kind, tw, dz, dx = place
            return gathered[kind, tw].at[pl.ds(row_of(dz, dx), ROWS), :]
        if what == "E":
            _, kind, tw, dz, dx = place
            return extras[kind, tw].at[pl.ds(pack_of(dz, dx), PACK), :]
        if what in sums:
            _, r0, nr, c0, nc = place
            return sums[what].at[pl.ds(r0, nr), pl.ds(c0, nc)]
        if what == "R":
            _, key, nr, nc = place
            return landing[nr, nc].at[R_SLOT[key]]
        if what == "W":
            _, dy, other, r0, nr = place
            return w3.at[pl.ds(r0, nr), shard(dy, other)]
        if what == "CX":
            _, dy, r0, nr = place
            return cx.at[dy, pl.ds(r0, nr), :]
        return yr[place[1][1]].at[Y_SLOT[place[1]]]

    copies = {}

    def copy_of(key):
        if key not in copies:
            m = MSGS[key]
            copies[key] = pltpu.make_async_remote_copy(
                src_ref=ref_of(m.src),
                dst_ref=ref_of(m.dst),
                send_sem=send_sem.at[INDEX[key]],
                recv_sem=recv_sem.at[INDEX[key]],
                device_id=peer[m.link],
                device_id_type=pl.DeviceIdType.MESH,
            )
        return copies[key]

    def pick():
        hits = ids[...] == 0
        chosen = jnp.sum(jnp.where(hits, 1.0, 0.0), axis=0, keepdims=True)
        share = jnp.sum(jnp.where(hits, probs[...], 0.0), axis=0, keepdims=True)
        above = lax.broadcasted_iota(jnp.int32, (TOK, TOK), 0) < lax.broadcasted_iota(jnp.int32, (TOK, TOK), 1)
        wide = jnp.broadcast_to(chosen, (TOK, TOK))
        slot = jnp.dot(
            wide.astype(BF), jnp.where(above, 1.0, 0.0).astype(BF), preferred_element_type=F32
        )
        row = lax.broadcasted_iota(jnp.int32, (TOK, TOK), 0).astype(F32)
        whole = jnp.where((slot == row) & (wide > 0.5), 1.0, 0.0)
        across_out[...] = whole[: ROWS + PACK].astype(BF)
        low = whole[ROWS : ROWS + PACK]
        r8 = lax.broadcasted_iota(jnp.int32, (PACK, TOK), 0)
        wanted = (r8 + (ROWS - EXTRA)).astype(F32)
        high = jnp.where((slot[:PACK] == wanted) & (wide[:PACK] > 0.5) & (r8 >= EXTRA), 1.0, 0.0)
        maps = [whole[:ROWS], low, high]
        shares = [jnp.sum(m * share, axis=1, keepdims=True) for m in maps]
        maps = [m.astype(BF) for m in maps]

        def take(k, source, c0, cols, scale):
            got = jnp.dot(maps[k], source[:, pl.ds(c0, cols)], preferred_element_type=F32)
            return got * shares[k] if scale else got

        for c0, cols, kind in ((0, CA, "A"), (CA, CB, "B")):
            for tw, source in ((0, tokens), (1, cot)):
                gathered[kind, tw][pl.ds(0, ROWS), :] = take(0, source, c0, cols, tw == 1).astype(BF)
                extras[kind, tw][pl.ds(0, PACK), :] = (
                    take(1, source, c0, cols // 2, tw == 1) + take(2, source, c0 + cols // 2, cols // 2, tw == 1)
                ).astype(BF)
        pl.semaphore_wait(barrier, len(peer))

    def spread(high, shape, axis):
        i = lax.broadcasted_iota(jnp.int32, shape, axis)
        j = lax.broadcasted_iota(jnp.int32, shape, 1 - axis)
        return jnp.where((i >> 2) * PACK + (i & 3) + (EXTRA if high else 0) == j, 1.0, 0.0).astype(BF)

    def weights():
        for load in loads:
            load.wait()

    nt = (((1,), (1,)), ((), ()))

    def main(*group):
        rows = pl.ds(row_of(group[0], 0), GROUP * len(group))
        spots = [
            (pl.ds(row_of(dz, 0) + NX * ROWS, NX * EXTRA), pl.ds(pack_of(dz, 0), NX * PACK)) for dz in group
        ]
        for kind, cols in (("A", CA // 2), ("B", CB // 2)):
            for tw in (0, 1):
                for high in (0, 1):
                    for tail, packed in spots:
                        gathered[kind, tw][tail, pl.ds(high * cols, cols)] = jnp.dot(
                            spread(high, (NX * EXTRA, NX * PACK), 0), extras[kind, tw][packed, :],
                            preferred_element_type=F32,
                        ).astype(BF)
        ra, rb, sa, sb = ga0[rows, :], gb0[rows, :], ga1[rows, :], gb1[rows, :]
        gate = jnp.dot(ra, wg[pl.ds(0, CA), :], preferred_element_type=F32) + jnp.dot(
            rb, wg[pl.ds(CA, CB), :], preferred_element_type=F32
        )
        up = jnp.dot(ra, wu[pl.ds(0, CA), :], preferred_element_type=F32) + jnp.dot(
            rb, wu[pl.ds(CA, CB), :], preferred_element_type=F32
        )
        back = lax.dot_general(sa, wd[:, pl.ds(0, CA)], nt, preferred_element_type=F32) + lax.dot_general(
            sb, wd[:, pl.ds(CA, CB)], nt, preferred_element_type=F32
        )
        sigma = jax.nn.sigmoid(gate)
        act = gate * sigma
        hid[rows, :] = (act * up).astype(BF)
        gb = (back * up * sigma * (1.0 + gate * (1.0 - sigma))).astype(BF)
        ub = (back * act).astype(BF)
        gback[rows, :] = gb
        uback[rows, :] = ub
        for c0 in range(0, D, 256):
            cols = pl.ds(c0, 256)
            part[rows, cols] = (
                lax.dot_general(gb, wg[cols, :], nt, preferred_element_type=F32)
                + lax.dot_general(ub, wu[cols, :], nt, preferred_element_type=F32)
            ).astype(BF)

        for out, c0, cols in ((pa, 0, CA // 2), (pb, CA, CB // 2)):
            for tail, packed in spots:
                out[packed, :] = sum(
                    jnp.dot(
                        spread(high, (NX * PACK, NX * EXTRA), 1), part[tail, pl.ds(c0 + high * cols, cols)],
                        preferred_element_type=F32,
                    )
                    for high in (0, 1)
                ).astype(BF)

    def add(key, what, r0, nr, c0, nc):
        got = landing[nr, nc].at[R_SLOT[key]]
        here = (pl.ds(r0, nr), pl.ds(c0, nc))
        sums[what][here] = sums[what][here] + got[...]

    cut = EARLY * GROUP
    halves = ((0, cut), (cut, NZ * GROUP - cut))

    def turn(late):
        rows = pl.ds(*halves[late])
        for i, source in enumerate((gback, uback, hid)):
            (turned1 if late else turned0)[pl.ds(i * H, H), :] = jnp.transpose(source[rows, :])

    def product(u, kind, i, late):
        return jnp.dot(
            (turned1 if late else turned0)[pl.ds(*UNITS[u]), :],
            gathered[kind, u][pl.ds(*halves[late]), pl.ds(i * 256, 256)],
            preferred_element_type=F32,
        )

    def tile(u, kind, i):
        return pl.ds(*UNITS[u]), pl.ds((0 if kind == "A" else CA) + i * 256, 256)

    def early(u, kind, i):
        acc[tile(u, kind, i)] = product(u, kind, i, 0)

    def grad(u, kind, i):
        here = tile(u, kind, i)
        w3[here] = (acc[here] + product(u, kind, i, 1)).astype(BF)

    def cadd(dy, r0, nr):
        here = (pl.ds(r0, nr), shard(dy, False))
        w3[here] = w3[here] + cx[dy, pl.ds(r0, nr), :]

    def yadd(key, dy, r0, nr):
        here = (pl.ds(r0, nr), shard(dy, False))
        w3[here] = w3[here] + yr[key[1]][Y_SLOT[key]]

    def final():
        ret_out[pl.ds(0, ROWS), :] = part[pl.ds(0, ROWS), :]
        for packed, c0, cols in ((pa, 0, CA // 2), (pb, CA, CB // 2)):
            for high in (0, 1):
                ret_out[pl.ds(ROWS, PACK), pl.ds(c0 + high * cols, cols)] = jnp.dot(
                    spread(high, (PACK, NX * PACK), 0), packed[pl.ds(0, NX * PACK), :],
                    preferred_element_type=F32,
                ).astype(BF)

    def wout():
        own = shard(0, False)
        g_out[...] = jnp.transpose(w3[pl.ds(0, H), own])
        u_out[...] = jnp.transpose(w3[pl.ds(H, H), own])
        d_out[...] = w3[pl.ds(2 * H, H), own]

    run = dict(early=early, pick=pick, weights=weights, main=main, add=add, turn=turn, grad=grad,
               cadd=cadd, yadd=yadd, final=final, wout=wout)
    arrived = set()
    for task in ORDER:
        for dep in task.deps:
            if dep in MSGS and dep not in arrived:
                copy_of(dep).wait_recv()
                arrived.add(dep)
        if task.emit is not None:
            run[task.emit[0]](*task.emit[1:])
        for key in task.sends:
            copy_of(key).start()
    for key in KEYS:
        copy_of(key).wait_send()


def per_device(tokens, cotangent, route_ids, route_probs, gate_weight, up_weight, down_weight):
    vmem = pl.BlockSpec(memory_space=pltpu.VMEM)
    anywhere = pl.BlockSpec(memory_space=pl.ANY)
    rows, packs = NZ * GROUP, NZ * NX * PACK
    scratch = [
        pltpu.VMEM((rows, CA), BF), pltpu.VMEM((rows, CA), BF),
        pltpu.VMEM((rows, CB), BF), pltpu.VMEM((rows, CB), BF),
        pltpu.VMEM((packs, CA // 2), BF), pltpu.VMEM((packs, CA // 2), BF),
        pltpu.VMEM((packs, CB // 2), BF), pltpu.VMEM((packs, CB // 2), BF),
        pltpu.VMEM((rows, D), BF),
        pltpu.VMEM((packs, CA // 2), BF), pltpu.VMEM((packs, CB // 2), BF),
        pltpu.VMEM((D, H), BF), pltpu.VMEM((D, H), BF), pltpu.VMEM((H, D), BF),
        pltpu.VMEM((rows, H), BF), pltpu.VMEM((rows, H), BF), pltpu.VMEM((rows, H), BF),
        pltpu.VMEM((3 * H, EARLY * GROUP), BF), pltpu.VMEM((3 * H, rows - EARLY * GROUP), BF),
        pltpu.VMEM((3 * H, D), F32),
        pltpu.VMEM((3 * H, D), BF),
        pltpu.VMEM((NY, 3 * H, SH), BF),
        *(pltpu.VMEM((len(Y_SLOT) // 2, nrows // 2, SH), BF) for _, nrows in UNITS),
    ]
    scratch += [pltpu.VMEM((R_COUNT[s],) + s, BF) for s in R_SHAPES]
    scratch += [
        pltpu.SemaphoreType.DMA((3,)),
        pltpu.SemaphoreType.DMA((len(KEYS),)),
        pltpu.SemaphoreType.DMA((len(KEYS),)),
    ]
    returned, across, gate_grad, up_grad, down_grad = pl.pallas_call(
        kernel,
        out_shape=(
            jax.ShapeDtypeStruct((ROWS + PACK, D), BF),
            jax.ShapeDtypeStruct((ROWS + PACK, TOK), BF),
            jax.ShapeDtypeStruct((SH, H), BF),
            jax.ShapeDtypeStruct((SH, H), BF),
            jax.ShapeDtypeStruct((H, SH), BF),
        ),
        in_specs=[vmem, vmem, vmem, vmem, anywhere, anywhere, anywhere],
        out_specs=(vmem,) * 5,
        scratch_shapes=scratch,
        compiler_params=pltpu.CompilerParams(
            collective_id=0, has_side_effects=True, vmem_limit_bytes=67043328
        ),
    )(route_ids.T, route_probs.T, tokens, cotangent, gate_weight, up_weight, down_weight)
    token_grad = lax.dot_general(
        across, returned, (((0,), (0,)), ((), ())), preferred_element_type=F32
    ).astype(BF)
    return token_grad, gate_grad, up_grad, down_grad


def solution(mesh):
    in_specs = (
        P(("dp", "expert"), None),
        P(("dp", "expert"), None),
        P(("dp", "expert"), None),
        P(("dp", "expert"), None),
        P(None, "expert"),
        P(None, "expert"),
        P("expert", None),
    )
    out_specs = (P(("dp", "expert"), None), P("dp", "expert"), P("dp", "expert"), P("expert", "dp"))
    return jax.shard_map(
        per_device, mesh=mesh, in_specs=in_specs, out_specs=out_specs, check_vma=False
    )
```

```python
import functools
import heapq

import jax
import jax.numpy as jnp
from jax import lax
from jax.experimental import pallas as pl
from jax.experimental.pallas import tpu as pltpu
from jax.sharding import PartitionSpec as P

CAP = 36
ROWS = 32
PACK = 8
EXTRA = CAP - ROWS
TOK = 128
D = 3072
H = 256
CA = 1280
CB = D - CA
NX, NZ, NY = 4, 8, 4
SH = D // 8
UNITS = ((0, 2 * H), (2 * H, H))
BF = jnp.bfloat16
F32 = jnp.float32
LINK_RATE = 46e3
CORE_RATE = 250e3
LATENCY = 1.6

REACH = {
    0: {"x": (2, 1), "z": (4, 3)},
    1: {"x": (1, 2), "z": (3, 4)},
}
SIZE = {"x": NX, "z": NZ, "y": NY}
RS_COLS = {
    ("A", 0): (0, CA // 2),
    ("A", 1): (CA // 2, CA // 2),
    ("B", 0): (CA, CB // 2),
    ("B", 1): (CA + CB // 2, CB // 2),
}


class Msg:
    def __init__(self, link, size, src, dst):
        self.link, self.size, self.src, self.dst = link, size, src, dst


class Task:
    def __init__(self, name, deps, sends=(), dur=0.0, rank=0, emit=None):
        self.name, self.deps, self.sends = name, tuple(deps), list(sends)
        self.dur, self.rank, self.emit = dur, rank, emit


GROUP = NX * CAP


PLACE = {dz: i for i, dz in enumerate((0, 1, 7, 2, 6, 3, 5, 4))}
EARLY = 5
BATCHES = ((0,), (1, 7), (2, 6), (3,), (5,), (4,))


def row_of(dz, dx):
    return PLACE[dz] * GROUP + dx * ROWS


def pack_of(dz, dx):
    return (dz * NX + dx) * PACK


def plan():
    msgs, tasks = {}, []

    first_sends, hold = [], []
    by_dz = {dz: [] for dz in range(NZ)}
    for kind, f, g, cols in (("A", "x", "z", CA), ("B", "z", "x", CB)):
        for tw in (0, 1):
            def at(cf, cg):
                dx, dz = (cf, cg) if f == "x" else (cg, cf)
                return dz % NZ, dx % NX

            def send(cf, cg, axis, up):
                step = -1 if up else 1
                nf, ng = (cf + step, cg) if axis == f else (cf, cg + step)
                dst = at(nf, ng)
                link = axis + ("+" if up else "-")
                keys = []
                for what, name, size in (("G", "ag", ROWS * cols), ("E", "age", PACK * cols // 2)):
                    key = (name, kind, tw) + dst
                    msgs[key] = Msg(link, size * 2, (what, kind, tw) + at(cf, cg), (what, kind, tw) + dst)
                    keys.append(key)
                by_dz[dst[0]].extend(keys)
                return keys

            def visit(cf, cg, via, up, hops):
                out = []
                if via in (None, f):
                    for u in (True, False):
                        reach = REACH[tw][f][0 if u else 1]
                        if via is None or (u == up and hops < reach):
                            out.append((send(cf, cg, f, u), cf + (-1 if u else 1), cg, f, u, 1 if via is None else hops + 1))
                    for u in (True, False):
                        out.append((send(cf, cg, g, u), cf, cg + (-1 if u else 1), g, u, 1))
                elif hops < REACH[tw][g][0 if up else 1]:
                    out.append((send(cf, cg, g, up), cf, cg + (-1 if up else 1), g, up, hops + 1))
                if via is None:
                    first_sends.extend(k for o in out for k in o[0])
                elif out:
                    here = (kind, tw) + at(cf, cg)
                    sends = [k for o in out for k in o[0]]
                    tasks.append(Task(("fwd",) + here, [("ag",) + here, ("age",) + here], sends, 0.05, 0))
                    if any(msgs[k].link[0] == "x" for k in sends):
                        hold.append(("fwd",) + here)
                for key, a, b, v, u, h in out:
                    visit(a, b, v, u, h)

            visit(0, 0, None, None, 0)
    tasks.append(Task("pick", [], first_sends, 2.0, 0, ("pick",)))

    for group in BATCHES:
        deps = ["pick", "weights"] + [k for dz in group for k in by_dz[dz]]
        dur = 2.5 + 2.0 * len(group)
        tasks.append(Task(("main", group[0]), deps, [], dur, 3, ("main",) + group))
        for dz in group[1:]:
            tasks.append(Task(("main", dz), [("main", group[0])], [], 0.0, 1))
    tasks.append(Task("weights", ["pick"], [], 0.1, 1, ("weights",)))
    task_of = {t.name: t for t in tasks}

    def chain(kind, tw, axis, up, fixed, at_of, blocks, ready, packed=False):
        c0, cols = RS_COLS[kind, tw]
        what, nrows = "P", ROWS * blocks
        if packed:
            what, nrows, c0, cols = "P" + kind, PACK * blocks, 0, (CA if kind == "A" else CB) // 2
        reach = REACH[tw][axis][0 if up else 1]
        sign = 1 if up else -1
        prev = None
        for k in range(reach, -1, -1):
            here = (sign * k) % SIZE[axis]
            r0 = pack_of(*at_of(here)) if packed else row_of(*at_of(here))
            name = ("rs", kind, tw, axis, up, fixed, packed, k)
            key = ("rsm", kind, tw, axis, up, fixed, packed, k - 1)
            deps = list(ready(here))
            if prev is not None:
                deps.append(prev)
            sends = []
            if k > 0:
                msgs[key] = Msg(
                    axis + ("+" if up else "-"), nrows * cols * 2, (what, r0, nrows, c0, cols), ("R", key, nrows, cols)
                )
                sends = [key]
            emit = None if prev is None else ("add", prev, what, r0, nrows, c0, cols)
            dur = 0.0 if prev is None else 0.1 + nrows * cols * 2 / 1.5e6
            tasks.append(Task(name, deps, sends, dur, 1 if k else 2, emit))
            prev = key
        return name

    later = {dz: [("main", 4)] if dz in (0, 1, 7) else [] for dz in range(NZ)}
    ends = []
    for tw, packed in ((0, False), (1, False), (0, True), (1, True)):
        if not (packed and tw == 1):
            za = {
                p: [
                    chain("A", tw, "z", up, p, lambda h, p=p: (h, p), 2, lambda h: [("main", h)], packed)
                    for up in (True, False)
                ]
                for p in (2, 0)
            }
            ends += [
                chain("A", tw, "x", up, 0, lambda h: (0, h), 1, lambda h: za[h // 2 * 2], packed)
                for up in (True, False)
            ]
        if packed and tw == 0:
            continue
        xb = {}
        for dz in (4, 3, 5, 2, 6, 1, 7, 0):
            xb[dz] = [
                chain(
                    "B", tw, "x", up, dz, lambda h, dz=dz: (dz, h), 1, lambda h, dz=dz: [("main", dz)] + hold + later[dz], packed
                )
                for up in (True, False)
            ]
        ends += [
            chain("B", tw, "z", up, 0, lambda h: (h, 0), 1, lambda h: xb[h], packed)
            for up in (True, False)
        ]
    tasks.append(Task("final", ends, [], 1.5, 5, ("final",)))

    mains = [("main", dz) for dz in range(NZ)]
    tasks.append(Task("turn early", [("main", dz) for dz in PLACE if PLACE[dz] < EARLY], [], 1.0, 4, ("turn", 0)))
    early = "turn early"
    for u, (r0, nrows) in enumerate(UNITS):
        for kind, count in (("A", CA // 256), ("B", CB // 256)):
            for i in range(count):
                tasks.append(Task(("early", u, kind, i), [early], [], 0.1 + nrows / 1200, 4, ("early", u, kind, i)))
                early = tasks[-1].name
    tasks.append(Task("turn", mains + [early], [], 0.7, 4, ("turn", 1)))
    last, dp_ends = "turn", []
    for u, (r0, nrows) in enumerate(UNITS):
        for kind, count in (("A", CA // 256), ("B", CB // 256)):
            for i in range(count):
                tasks.append(Task(("grad", u, kind, i), [last], [], 0.1 + nrows / 1500, 4, ("grad", u, kind, i)))
                last = tasks[-1].name
        for dy in (2, 3, 1, 0):
            msgs["cx", u, dy] = Msg("core", nrows * SH * 2, ("W", dy, True, r0, nrows), ("CX", dy, r0, nrows))
            tasks[-1].sends.append(("cx", u, dy))
        for dy in (2, 3, 1, 0):
            tasks.append(Task(("cadd", u, dy), [last, ("cx", u, dy)], [], 0.1 + nrows / 1500, 2, ("cadd", dy, r0, nrows)))
        half = nrows // 2
        for tw in (0, 1):
            for up in (True, False):
                reach = REACH[tw]["x"][0 if up else 1]
                prev = None
                for k in range(reach, -1, -1):
                    dy = (k if up else -k) % NY
                    name = ("y", u, tw, up, k)
                    key = ("ym", u, tw, up, k - 1)
                    place = (dy, r0 + tw * half, half)
                    deps = [("cadd", u, dy)] + ([prev] if prev else [])
                    sends = []
                    if k > 0:
                        msgs[key] = Msg(
                            "y" + ("+" if up else "-"), half * SH * 2, ("W", dy, False) + place[1:], ("Y", key)
                        )
                        sends = [key]
                    emit = None if prev is None else ("yadd", prev) + place
                    tasks.append(Task(name, deps, sends, 0.0 if prev is None else 0.1 + half / 1500, 2, emit))
                    prev = key
                dp_ends.append(name)
    tasks.append(Task("wout", dp_ends, [], 0.3, 5, ("wout",)))
    return msgs, schedule(msgs, tasks)


def schedule(msgs, tasks):
    waiting = {i: set(t.deps) for i, t in enumerate(tasks)}
    users = {}
    for i, t in enumerate(tasks):
        for d in t.deps:
            users.setdefault(d, []).append(i)
    tail = {}

    def tail_of(key):
        if key not in tail:
            tail[key] = 0.0
            for i in users.get(key, ()):
                t = tasks[i]
                sent = max([msgs[k].size / LINK_RATE + LATENCY + tail_of(k) for k in t.sends], default=0.0)
                tail[key] = max(tail[key], t.dur + max(sent, tail_of(t.name)))
        return tail[key]

    for t in tasks:
        sent = max([msgs[k].size / LINK_RATE + LATENCY + tail_of(k) for k in t.sends], default=0.0)
        t.tail = max(sent, tail_of(t.name))
    ready, arrivals, free, now, order = [], [], {}, 0.0, []
    times = {}

    def satisfy(key):
        for i in users.get(key, ()):
            waiting[i].discard(key)
            if not waiting[i]:
                heapq.heappush(ready, (tasks[i].rank, -tasks[i].tail, i))

    for i in range(len(tasks)):
        if not waiting[i]:
            heapq.heappush(ready, (tasks[i].rank, -tasks[i].tail, i))
    seq = 0
    while ready or arrivals:
        while arrivals and arrivals[0][0] <= now:
            satisfy(heapq.heappop(arrivals)[2])
        if not ready:
            now = arrivals[0][0]
            continue
        i = heapq.heappop(ready)[2]
        t = tasks[i]
        now += t.dur
        order.append(t)
        times[t.name] = now
        for key in t.sends:
            m = msgs[key]
            start = max(now, free.get(m.link, 0.0))
            rate = CORE_RATE if m.link == "core" else LINK_RATE
            free[m.link] = start + m.size / rate
            seq += 1
            heapq.heappush(arrivals, (free[m.link] + LATENCY, seq, key))
        satisfy(t.name)
    if len(order) != len(tasks):
        raise ValueError("stuck")
    plan.times, plan.end = times, now
    return order


MSGS, ORDER = plan()
KEYS = sorted(MSGS, key=repr)
INDEX = {k: i for i, k in enumerate(KEYS)}
R_SLOT, R_COUNT = {}, {}
for _k in KEYS:
    if _k[0] == "rsm":
        _, _, _nr, _nc = MSGS[_k].dst
        R_SLOT[_k] = R_COUNT.get((_nr, _nc), 0)
        R_COUNT[_nr, _nc] = R_SLOT[_k] + 1
R_SHAPES = sorted(R_COUNT)
Y_SLOT = {}
for _k in KEYS:
    if _k[0] == "ym":
        Y_SLOT[_k] = sum(o[1] == _k[1] for o in Y_SLOT)


def kernel(ids, probs, tokens, cot, wg_hbm, wu_hbm, wd_hbm, ret_out, across_out, g_out, u_out, d_out,
           ga0, ga1, gb0, gb1, ea0, ea1, eb0, eb1, part, pa, pb, wg, wu, wd, gback, uback, hid, turned0, turned1, acc, w3, cx, yr0, yr1, *rest):
    landing = dict(zip(R_SHAPES, rest[: len(R_SHAPES)]))
    wsem, send_sem, recv_sem = rest[len(R_SHAPES):]
    gathered = {("A", 0): ga0, ("A", 1): ga1, ("B", 0): gb0, ("B", 1): gb1}
    extras = {("A", 0): ea0, ("A", 1): ea1, ("B", 0): eb0, ("B", 1): eb1}
    yr = (yr0, yr1)
    sums = {"P": part, "PA": pa, "PB": pb}

    e = lax.axis_index("expert")
    d = lax.axis_index("dp")
    x, z, y, c = e // NZ, e % NZ, d // 2, d % 2
    peer = {
        "z+": {"expert": x * NZ + (z + 1) % NZ},
        "z-": {"expert": x * NZ + (z + NZ - 1) % NZ},
        "x+": {"expert": ((x + 1) % NX) * NZ + z},
        "x-": {"expert": ((x + NX - 1) % NX) * NZ + z},
        "y+": {"dp": ((y + 1) % NY) * 2 + c},
        "y-": {"dp": ((y + NY - 1) % NY) * 2 + c},
        "core": {"dp": y * 2 + 1 - c},
    }
    loads = [
        pltpu.make_async_copy(src, dst, wsem.at[i])
        for i, (src, dst) in enumerate(((wg_hbm, wg), (wu_hbm, wu), (wd_hbm, wd)))
    ]
    for load in loads:
        load.start()
    barrier = pltpu.get_barrier_semaphore()
    for target in peer.values():
        pl.semaphore_signal(barrier, inc=1, device_id=target, device_id_type=pl.DeviceIdType.MESH)

    def shard(dy, other):
        owner = ((y + dy) % NY) * 2 + (1 - c if other else c)
        return pl.ds(pl.multiple_of(owner * SH, 128), SH)

    def ref_of(place):
        what = place[0]
        if what == "G":
            _, kind, tw, dz, dx = place
            return gathered[kind, tw].at[pl.ds(row_of(dz, dx), ROWS), :]
        if what == "E":
            _, kind, tw, dz, dx = place
            return extras[kind, tw].at[pl.ds(pack_of(dz, dx), PACK), :]
        if what in sums:
            _, r0, nr, c0, nc = place
            return sums[what].at[pl.ds(r0, nr), pl.ds(c0, nc)]
        if what == "R":
            _, key, nr, nc = place
            return landing[nr, nc].at[R_SLOT[key]]
        if what == "W":
            _, dy, other, r0, nr = place
            return w3.at[pl.ds(r0, nr), shard(dy, other)]
        if what == "CX":
            _, dy, r0, nr = place
            return cx.at[dy, pl.ds(r0, nr), :]
        return yr[place[1][1]].at[Y_SLOT[place[1]]]

    copies = {}

    def copy_of(key):
        if key not in copies:
            m = MSGS[key]
            copies[key] = pltpu.make_async_remote_copy(
                src_ref=ref_of(m.src),
                dst_ref=ref_of(m.dst),
                send_sem=send_sem.at[INDEX[key]],
                recv_sem=recv_sem.at[INDEX[key]],
                device_id=peer[m.link],
                device_id_type=pl.DeviceIdType.MESH,
            )
        return copies[key]

    def pick():
        hits = ids[...] == 0
        chosen = jnp.sum(jnp.where(hits, 1.0, 0.0), axis=0, keepdims=True)
        share = jnp.sum(jnp.where(hits, probs[...], 0.0), axis=0, keepdims=True)
        above = lax.broadcasted_iota(jnp.int32, (TOK, TOK), 0) < lax.broadcasted_iota(jnp.int32, (TOK, TOK), 1)
        wide = jnp.broadcast_to(chosen, (TOK, TOK))
        slot = jnp.dot(
            wide.astype(BF), jnp.where(above, 1.0, 0.0).astype(BF), preferred_element_type=F32
        )
        row = lax.broadcasted_iota(jnp.int32, (TOK, TOK), 0).astype(F32)
        whole = jnp.where((slot == row) & (wide > 0.5), 1.0, 0.0)
        across_out[...] = whole[: ROWS + PACK].astype(BF)
        low = whole[ROWS : ROWS + PACK]
        r8 = lax.broadcasted_iota(jnp.int32, (PACK, TOK), 0)
        wanted = (r8 + (ROWS - EXTRA)).astype(F32)
        high = jnp.where((slot[:PACK] == wanted) & (wide[:PACK] > 0.5) & (r8 >= EXTRA), 1.0, 0.0)
        maps = [whole[:ROWS], low, high]
        shares = [jnp.sum(m * share, axis=1, keepdims=True) for m in maps]
        maps = [m.astype(BF) for m in maps]

        def take(k, source, c0, cols, scale):
            got = jnp.dot(maps[k], source[:, pl.ds(c0, cols)], preferred_element_type=F32)
            return got * shares[k] if scale else got

        for c0, cols, kind in ((0, CA, "A"), (CA, CB, "B")):
            for tw, source in ((0, tokens), (1, cot)):
                gathered[kind, tw][pl.ds(0, ROWS), :] = take(0, source, c0, cols, tw == 1).astype(BF)
                extras[kind, tw][pl.ds(0, PACK), :] = (
                    take(1, source, c0, cols // 2, tw == 1) + take(2, source, c0 + cols // 2, cols // 2, tw == 1)
                ).astype(BF)
        pl.semaphore_wait(barrier, len(peer))

    def spread(high, shape, axis):
        i = lax.broadcasted_iota(jnp.int32, shape, axis)
        j = lax.broadcasted_iota(jnp.int32, shape, 1 - axis)
        return jnp.where((i >> 2) * PACK + (i & 3) + (EXTRA if high else 0) == j, 1.0, 0.0).astype(BF)

    def weights():
        for load in loads:
            load.wait()

    nt = (((1,), (1,)), ((), ()))

    def main(*group):
        rows = pl.ds(row_of(group[0], 0), GROUP * len(group))
        spots = [
            (pl.ds(row_of(dz, 0) + NX * ROWS, NX * EXTRA), pl.ds(pack_of(dz, 0), NX * PACK)) for dz in group
        ]
        for kind, cols in (("A", CA // 2), ("B", CB // 2)):
            for tw in (0, 1):
                for high in (0, 1):
                    for tail, packed in spots:
                        gathered[kind, tw][tail, pl.ds(high * cols, cols)] = jnp.dot(
                            spread(high, (NX * EXTRA, NX * PACK), 0), extras[kind, tw][packed, :],
                            preferred_element_type=F32,
                        ).astype(BF)
        ra, rb, sa, sb = ga0[rows, :], gb0[rows, :], ga1[rows, :], gb1[rows, :]
        gate = jnp.dot(ra, wg[pl.ds(0, CA), :], preferred_element_type=F32) + jnp.dot(
            rb, wg[pl.ds(CA, CB), :], preferred_element_type=F32
        )
        up = jnp.dot(ra, wu[pl.ds(0, CA), :], preferred_element_type=F32) + jnp.dot(
            rb, wu[pl.ds(CA, CB), :], preferred_element_type=F32
        )
        back = lax.dot_general(sa, wd[:, pl.ds(0, CA)], nt, preferred_element_type=F32) + lax.dot_general(
            sb, wd[:, pl.ds(CA, CB)], nt, preferred_element_type=F32
        )
        sigma = jax.nn.sigmoid(gate)
        act = gate * sigma
        hid[rows, :] = (act * up).astype(BF)
        gb = (back * up * sigma * (1.0 + gate * (1.0 - sigma))).astype(BF)
        ub = (back * act).astype(BF)
        gback[rows, :] = gb
        uback[rows, :] = ub
        for c0 in range(0, D, 256):
            cols = pl.ds(c0, 256)
            part[rows, cols] = (
                lax.dot_general(gb, wg[cols, :], nt, preferred_element_type=F32)
                + lax.dot_general(ub, wu[cols, :], nt, preferred_element_type=F32)
            ).astype(BF)

        for out, c0, cols in ((pa, 0, CA // 2), (pb, CA, CB // 2)):
            for tail, packed in spots:
                out[packed, :] = sum(
                    jnp.dot(
                        spread(high, (NX * PACK, NX * EXTRA), 1), part[tail, pl.ds(c0 + high * cols, cols)],
                        preferred_element_type=F32,
                    )
                    for high in (0, 1)
                ).astype(BF)

    def add(key, what, r0, nr, c0, nc):
        got = landing[nr, nc].at[R_SLOT[key]]
        here = (pl.ds(r0, nr), pl.ds(c0, nc))
        sums[what][here] = sums[what][here] + got[...]

    cut = EARLY * GROUP
    halves = ((0, cut), (cut, NZ * GROUP - cut))

    def turn(late):
        rows = pl.ds(*halves[late])
        for i, source in enumerate((gback, uback, hid)):
            (turned1 if late else turned0)[pl.ds(i * H, H), :] = jnp.transpose(source[rows, :])

    def product(u, kind, i, late):
        return jnp.dot(
            (turned1 if late else turned0)[pl.ds(*UNITS[u]), :],
            gathered[kind, u][pl.ds(*halves[late]), pl.ds(i * 256, 256)],
            preferred_element_type=F32,
        )

    def tile(u, kind, i):
        return pl.ds(*UNITS[u]), pl.ds((0 if kind == "A" else CA) + i * 256, 256)

    def early(u, kind, i):
        acc[tile(u, kind, i)] = product(u, kind, i, 0)

    def grad(u, kind, i):
        here = tile(u, kind, i)
        w3[here] = (acc[here] + product(u, kind, i, 1)).astype(BF)

    def cadd(dy, r0, nr):
        here = (pl.ds(r0, nr), shard(dy, False))
        w3[here] = w3[here] + cx[dy, pl.ds(r0, nr), :]

    def yadd(key, dy, r0, nr):
        here = (pl.ds(r0, nr), shard(dy, False))
        w3[here] = w3[here] + yr[key[1]][Y_SLOT[key]]

    def final():
        ret_out[pl.ds(0, ROWS), :] = part[pl.ds(0, ROWS), :]
        for packed, c0, cols in ((pa, 0, CA // 2), (pb, CA, CB // 2)):
            for high in (0, 1):
                ret_out[pl.ds(ROWS, PACK), pl.ds(c0 + high * cols, cols)] = jnp.dot(
                    spread(high, (PACK, NX * PACK), 0), packed[pl.ds(0, NX * PACK), :],
                    preferred_element_type=F32,
                ).astype(BF)

    def wout():
        own = shard(0, False)
        g_out[...] = jnp.transpose(w3[pl.ds(0, H), own])
        u_out[...] = jnp.transpose(w3[pl.ds(H, H), own])
        d_out[...] = w3[pl.ds(2 * H, H), own]

    run = dict(early=early, pick=pick, weights=weights, main=main, add=add, turn=turn, grad=grad,
               cadd=cadd, yadd=yadd, final=final, wout=wout)
    arrived = set()
    for task in ORDER:
        for dep in task.deps:
            if dep in MSGS and dep not in arrived:
                copy_of(dep).wait_recv()
                arrived.add(dep)
        if task.emit is not None:
            run[task.emit[0]](*task.emit[1:])
        for key in task.sends:
            copy_of(key).start()
    for key in KEYS:
        copy_of(key).wait_send()


def per_device(tokens, cotangent, route_ids, route_probs, gate_weight, up_weight, down_weight):
    vmem = pl.BlockSpec(memory_space=pltpu.VMEM)
    anywhere = pl.BlockSpec(memory_space=pl.ANY)
    rows, packs = NZ * GROUP, NZ * NX * PACK
    scratch = [
        pltpu.VMEM((rows, CA), BF), pltpu.VMEM((rows, CA), BF),
        pltpu.VMEM((rows, CB), BF), pltpu.VMEM((rows, CB), BF),
        pltpu.VMEM((packs, CA // 2), BF), pltpu.VMEM((packs, CA // 2), BF),
        pltpu.VMEM((packs, CB // 2), BF), pltpu.VMEM((packs, CB // 2), BF),
        pltpu.VMEM((rows, D), BF),
        pltpu.VMEM((packs, CA // 2), BF), pltpu.VMEM((packs, CB // 2), BF),
        pltpu.VMEM((D, H), BF), pltpu.VMEM((D, H), BF), pltpu.VMEM((H, D), BF),
        pltpu.VMEM((rows, H), BF), pltpu.VMEM((rows, H), BF), pltpu.VMEM((rows, H), BF),
        pltpu.VMEM((3 * H, EARLY * GROUP), BF), pltpu.VMEM((3 * H, rows - EARLY * GROUP), BF),
        pltpu.VMEM((3 * H, D), F32),
        pltpu.VMEM((3 * H, D), BF),
        pltpu.VMEM((NY, 3 * H, SH), BF),
        *(pltpu.VMEM((len(Y_SLOT) // 2, nrows // 2, SH), BF) for _, nrows in UNITS),
    ]
    scratch += [pltpu.VMEM((R_COUNT[s],) + s, BF) for s in R_SHAPES]
    scratch += [
        pltpu.SemaphoreType.DMA((3,)),
        pltpu.SemaphoreType.DMA((len(KEYS),)),
        pltpu.SemaphoreType.DMA((len(KEYS),)),
    ]
    returned, across, gate_grad, up_grad, down_grad = pl.pallas_call(
        kernel,
        out_shape=(
            jax.ShapeDtypeStruct((ROWS + PACK, D), BF),
            jax.ShapeDtypeStruct((ROWS + PACK, TOK), BF),
            jax.ShapeDtypeStruct((SH, H), BF),
            jax.ShapeDtypeStruct((SH, H), BF),
            jax.ShapeDtypeStruct((H, SH), BF),
        ),
        in_specs=[vmem, vmem, vmem, vmem, anywhere, anywhere, anywhere],
        out_specs=(vmem,) * 5,
        scratch_shapes=scratch,
        compiler_params=pltpu.CompilerParams(
            collective_id=0, has_side_effects=True, vmem_limit_bytes=67043328
        ),
    )(route_ids.T, route_probs.T, tokens, cotangent, gate_weight, up_weight, down_weight)
    token_grad = lax.dot_general(
        across, returned, (((0,), (0,)), ((), ())), preferred_element_type=F32
    ).astype(BF)
    return token_grad, gate_grad, up_grad, down_grad


def solution(mesh):
    in_specs = (
        P(("dp", "expert"), None),
        P(("dp", "expert"), None),
        P(("dp", "expert"), None),
        P(("dp", "expert"), None),
        P(None, "expert"),
        P(None, "expert"),
        P("expert", None),
    )
    out_specs = (P(("dp", "expert"), None), P("dp", "expert"), P("dp", "expert"), P("expert", "dp"))
    return jax.shard_map(
        per_device, mesh=mesh, in_specs=in_specs, out_specs=out_specs, check_vma=False
    )
```
